256 devices in a mesh: grp: 2 (over core), gx: 16 (over y, z_lo), gy: 8 (over z_hi, x).
Axes of the slice: x: 4, y: 4, z: 8 (z_hi: 2, z_lo: 4; z = z_hi * 4 + z_lo), core: 2. Of those that a mesh axis runs over, the one named last changes fastest.
Arguments:
- fields: float32 [2, 128, 256, 512], P('grp', 'gx', 'gy'), may hold values from -6 to 6
- stored: float32 [2, 128, 256, 512], P('grp', 'gx', 'gy'), may hold values from -6 to 6
- porosity: float32 [128, 256, 512], P('gx', 'gy'), may hold values from 0.1 to 0.9
- labels: int32 [128, 256, 512], P('gx', 'gy'), may hold values from 0 to 2
- heat_source: float32 [128, 256, 512], P('gx', 'gy'), may hold values from -6 to 6
- design_owner: int32 [128, 256, 512], P('gx', 'gy'), may hold values from 0 to 16383, as said below
Outputs:
- fields_out: float32 [2, 128, 256, 512], P('grp', 'gx', 'gy')
- sensitivity: float32 [16384], P(('grp', 'gx', 'gy'))
The draws below stay inside these ranges and needn't reach their ends.
Inputs may be any that keep to these rules, and one draw needn't show every extreme that they name: `design_owner`: each design cell is a contiguous block of 8 x 32 x 512 // 128 cells, aligned to those sizes; every design cell occurs.
All inputs are finite; a program needn't handle non-finite values.
Results may differ from the reference program's by a relative error of at most 0.00002.
Values sent between devices are 32-bit elements; how exact they have to be, the bound alone decides.
A program may use at most 64 MiB of HBM per device.

```python
import jax
import jax.numpy as jnp
from jax import lax

CX = 8
CY = 32
CZ = 512
ND_DEV = 64
STEPS = 2
NX = 128
NY = 256
NZ = 512
ND = 16384


def draw_design_owner(key, part):
    slab_depth = CZ // (2 * ND_DEV)
    slabs = 2 * ND_DEV
    tiles_y = NY // CY
    shape = (NX, NY, NZ)
    index_x = lax.broadcasted_iota(jnp.int32, shape, 0) // CX
    index_y = lax.broadcasted_iota(jnp.int32, shape, 1) // CY
    index_z = lax.broadcasted_iota(jnp.int32, shape, 2) // slab_depth
    block_number = (index_x * tiles_y + index_y) * slabs + index_z
    shuffled = jax.random.permutation(jax.random.fold_in(key, 17), ND).astype(jnp.int32)
    return shuffled[block_number].astype(jnp.int32)


def place_ends(result, key, least, high):
    longest = result.shape.index(max(result.shape))
    spots = []
    for shift in (0, 1):
        where = [jax.random.randint(jax.random.fold_in(key, axis), (), 0, length) for axis, length in enumerate(result.shape)]
        where[longest] = (where[longest] + shift) % result.shape[longest]
        spots.append(tuple(where))
    return result.at[spots[0]].set(least).at[spots[1]].set(high)


def levels(own_key, shape, shards, least, largest):
    def one(dim, blocks):
        heights = jax.random.uniform(jax.random.fold_in(jax.random.fold_in(own_key, 6), dim), (blocks,), jnp.float32, least / len(shards), largest / len(shards))
        return jnp.repeat(jnp.exp(heights), shape[dim] // blocks).reshape((-1,) + (1,) * (len(shape) - dim - 1))

    loudness = one(*shards[0])
    for cut in shards[1:]:
        loudness = loudness * one(*cut)
    return loudness


def noise(stream_key, extent, width, reach, pieces=(), kind=jnp.bfloat16):
    gain = levels(stream_key, extent, pieces, -0.22, 0.18) if pieces else 1.0
    entries = jax.random.normal(stream_key, extent, jnp.float32) * width * gain
    return jnp.minimum(jnp.maximum(entries, -reach), reach).astype(kind)


def setup_inputs(seed: int = 0) -> dict:
    key_list = jax.random.split(jax.random.key(seed), 7)
    return {
        "fields": noise(key_list[0], (2, NX, NY, NZ), 1.0, 6.0, ((0, 2), (1, 16), (2, 8)), jnp.float32),
        "stored": noise(key_list[1], (2, NX, NY, NZ), 1.0, 6.0, ((0, 2), (1, 16), (2, 8)), jnp.float32),
        "porosity": jnp.clip(0.1 + 0.79999997 * jax.random.uniform(key_list[2], (NX, NY, NZ), jnp.float32) ** levels(key_list[2], (NX, NY, NZ), ((0, 16), (1, 8)), -0.2, 0.2), 0.1, 0.9),
        "labels": place_ends(jax.random.randint(key_list[3], (NX, NY, NZ), 0, 3), jax.random.fold_in(key_list[3], 1), 0, 2).astype(jnp.int32),
        "heat_source": noise(key_list[4], (NX, NY, NZ), 1.0, 6.0, ((0, 16), (1, 8)), jnp.float32),
        "design_owner": draw_design_owner(jax.random.fold_in(key_list[6], 71), 0),
    }


CONDUCT_SOLID = 1.0
CONDUCT_FLUID = 0.2
SOFTENING = 0.1
COOLING_RATE = 0.5
TIME_STEP = 0.08
MISFIT_WEIGHT = 1.0

def coefficients(porosity, labels):
    solid_mask = (labels == 0).astype(jnp.float32)
    fluid_mask = (labels == 1).astype(jnp.float32)
    porous_mask = (labels == 2).astype(jnp.float32)
    kappa_base = solid_mask * CONDUCT_SOLID + fluid_mask * CONDUCT_FLUID + porous_mask * (porosity * CONDUCT_SOLID + (1.0 - porosity) * CONDUCT_FLUID)
    kappa_slope = (solid_mask + porous_mask * porosity) * (CONDUCT_SOLID * SOFTENING)
    cooling = COOLING_RATE * (fluid_mask + porous_mask * (1.0 - porosity))
    return (kappa_base, kappa_slope, cooling)

def neighbours(padded):
    return [padded[2:, 1:-1, 1:-1], padded[:-2, 1:-1, 1:-1], padded[1:-1, 2:, 1:-1], padded[1:-1, :-2, 1:-1], padded[1:-1, 1:-1, 2:], padded[1:-1, 1:-1, :-2]]

def advance(field, porosity, labels, heat_source):
    kappa_base, kappa_slope, cooling = coefficients(porosity, labels)
    kappa = kappa_base + kappa_slope * field
    near_field = neighbours(jnp.pad(field, 1))
    near_kappa = neighbours(jnp.pad(kappa, 1))
    flux = jnp.zeros_like(field)
    for value_near, kappa_near in zip(near_field, near_kappa):
        flux = flux + 0.5 * (kappa + kappa_near) * (value_near - field)
    return field + TIME_STEP * (flux + heat_source - cooling * field)

def reference(fields, stored, porosity, labels, heat_source, design_owner):

    def stepper(field, density):
        return advance(field, density, labels, heat_source)
    state = fields[0]
    for step_index in range(STEPS):
        state = stepper(state, porosity)
    saved = [stored[0]]
    for step_index in range(STEPS - 1):
        saved.append(stepper(saved[-1], porosity))
    costate = fields[1]
    cell_grad = jnp.zeros_like(porosity)
    for step_index in range(STEPS - 1, -1, -1):
        pulled = jax.vjp(stepper, saved[step_index], porosity)[1](costate)
        costate = pulled[0] + MISFIT_WEIGHT * (saved[step_index] - stored[1])
        cell_grad = cell_grad + pulled[1]
    sensitivity = jax.ops.segment_sum(cell_grad.reshape(-1), design_owner.reshape(-1), num_segments=ND)
    return (jnp.stack([state, costate]), sensitivity)
```

```python
import jax
import jax.numpy as jnp
from jax import lax
from jax.experimental import pallas as pl
from jax.experimental.pallas import tpu as pltpu
from jax.sharding import PartitionSpec as P

MESH = pl.DeviceIdType.MESH
F32 = jnp.float32
YN, ZLN, ZHN, XN = 4, 4, 2, 4
NGX, NGY = YN * ZLN, ZHN * XN
ZN, CN = ZLN * ZHN, YN * XN
CX, CY, CZ = 8, 32, 512
KT = CZ // 128
Y0 = 8
YP = 48
PAD = (CX + 2, KT, YP, 128)
FLAT = (CX, KT, CY, 128)
ND_DEV = 64
OUTSIDE = -0.25

R_V0, R_P, R_L2, R_V1, R_L1 = 0, 4, 8, 12, 16
R_BULK, R_O1, R_O2, R_D1, R_D2 = 20, 21, 22, 23, 24
N_RECV = 25
N_SEND = 48


def interior(ref):
    return ref.at[pl.ds(1, CX), :, pl.ds(Y0, CY), :]


def faces(ref):
    return (
        (ref.at[pl.ds(CX, 1), :, pl.ds(Y0, CY), :], ref.at[pl.ds(0, 1), :, pl.ds(Y0, CY), :]),
        (ref.at[pl.ds(1, 1), :, pl.ds(Y0, CY), :], ref.at[pl.ds(CX + 1, 1), :, pl.ds(Y0, CY), :]),
        (ref.at[pl.ds(1, CX), :, pl.ds(Y0 + CY - 1, 1), :], ref.at[pl.ds(1, CX), :, pl.ds(Y0 - 1, 1), :]),
        (ref.at[pl.ds(1, CX), :, pl.ds(Y0, 1), :], ref.at[pl.ds(1, CX), :, pl.ds(Y0 + CY, 1), :]),
    )


def kernel(
    fields, stored, por, lab, heat, own,
    out, sens,
    V0, V1, KA, Q, L2, L1, S0, LB, PR, HT, RES,
    OB, ocol, otab, dcol, dtab, acc, sel,
    ssem, rsem, dsem, lsem,
):
    grp = lax.axis_index("grp")
    gx = lax.axis_index("gx")
    gy = lax.axis_index("gy")
    fwd = grp == 0
    adj = grp == 1
    yy, zl = gx // ZLN, lax.rem(gx, ZLN)
    zh, xx = gy // XN, lax.rem(gy, XN)
    zz = zh * ZLN + zl
    cc = yy * XN + xx
    has = (gx > 0, gx < NGX - 1, gy > 0, gy < NGY - 1)
    sends_to = (has[1], has[0], has[3], has[2])

    def device(g, step):
        dx, dy = ((1, 0), (-1, 0), (0, 1), (0, -1))[step]
        return {"grp": g, "gx": lax.rem(gx + dx + NGX, NGX), "gy": lax.rem(gy + dy + NGY, NGY)}

    def z_peer(d):
        z = lax.rem(zz + d, ZN)
        return {"grp": grp, "gx": yy * ZLN + lax.rem(z, ZLN), "gy": (z // ZLN) * XN + xx}

    def plane_peer(g, d):
        c = lax.rem(cc + d, CN)
        return {"grp": g, "gx": (c // XN) * ZLN + zl, "gy": zh * XN + lax.rem(c, XN)}

    partner = {"grp": 1 - grp, "gx": gx, "gy": gy}

    loads = []

    def load(src, dst, slot):
        for k in range(KT):
            c = pltpu.make_async_copy(src.at[:, :, pl.ds(128 * k, 128)], dst(k), lsem.at[slot, k])
            c.start()
            loads.append(c)
        return loads[-KT:]

    ld_stored = load(stored.at[0], lambda k: S0.at[:, k], 0)
    ld_lab = load(lab, lambda k: LB.at[:, k], 1)
    ld_por = load(por, lambda k: PR.at[:, k], 2)

    def fields_copies(dst, slot):
        return [
            pltpu.make_async_copy(
                fields.at[0, :, :, pl.ds(128 * k, 128)],
                dst.at[pl.ds(1, CX), k, pl.ds(Y0, CY), :],
                lsem.at[slot, k],
            )
            for k in range(KT)
        ]

    @pl.when(fwd)
    def _():
        for c in fields_copies(V0, 3):
            c.start()

    @pl.when(adj)
    def _():
        for c in fields_copies(L2, 3):
            c.start()

    ld_heat = load(heat, lambda k: HT.at[:, k], 4)
    ld_own = pltpu.make_async_copy(own.at[0, pl.ds(0, 8), :], OB, lsem.at[5, 0])
    ld_own.start()

    bar = pltpu.get_barrier_semaphore()

    def tell(dev):
        pl.semaphore_signal(bar, inc=1, device_id=dev, device_id_type=MESH)

    for s in range(4):

        @pl.when(sends_to[s])
        def _():
            tell(device(grp, s))

        @pl.when(jnp.logical_and(adj, sends_to[s]))
        def _():
            tell(device(0, s))

    tell(partner)
    for d in range(1, ZN):
        tell(z_peer(d))
    for d in range(1, CN):
        tell(plane_peer(grp, d))

    @pl.when(fwd)
    def _():
        for d in range(1, CN):
            tell(plane_peer(1, d))

    near = sum(h.astype(jnp.int32) for h in has)

    for s in range(4):

        @pl.when(jnp.logical_not(has[s]))
        def _():
            for ref, fill in ((V0, 0.0), (V1, 0.0), (Q, OUTSIDE), (L2, 0.0), (L1, 0.0)):
                if s == 0:
                    ref[0, :, pl.ds(Y0, CY), :] = jnp.full((KT, CY, 128), fill, F32)
                elif s == 1:
                    ref[CX + 1, :, pl.ds(Y0, CY), :] = jnp.full((KT, CY, 128), fill, F32)
                elif s == 2:
                    ref[pl.ds(1, CX), :, pl.ds(Y0 - 1, 1), :] = jnp.full((CX, KT, 1, 128), fill, F32)
                else:
                    ref[pl.ds(1, CX), :, pl.ds(Y0 + CY, 1), :] = jnp.full((CX, KT, 1, 128), fill, F32)

    for c in ld_lab + ld_por:
        c.wait()

    def solid_share(i, _):
        label = LB[i]
        q = jnp.where(label == 0, 1.0, jnp.where(label == 1, 0.0, PR[i]))
        Q[i + 1, :, pl.ds(Y0, CY), :] = q
        return 0

    lax.fori_loop(0, CX, solid_share, 0)
    for c in ld_stored:
        c.wait()

    sent = []

    def remote(cond, src, dst, dev, recv, send=None):
        slot = len(sent)

        def make():
            return pltpu.make_async_remote_copy(
                src_ref=src, dst_ref=dst, send_sem=ssem.at[slot], recv_sem=rsem.at[recv],
                device_id=dev, device_id_type=MESH,
            )

        @pl.when(cond)
        def _():
            make().start()

        sent.append((cond, make))

    def arrive(cond, dst, recv):
        @pl.when(cond)
        def _():
            pltpu.make_async_copy(dst, dst, rsem.at[recv]).wait()

    pl.semaphore_wait(bar, jnp.where(fwd, 2 * near + 1 + ZN - 1 + CN - 1, near + 1 + ZN - 1 + 2 * (CN - 1)))

    stored_faces = (
        S0.at[pl.ds(CX - 1, 1)], S0.at[pl.ds(0, 1)],
        S0.at[:, :, pl.ds(CY - 1, 1), :], S0.at[:, :, pl.ds(0, 1), :],
    )
    for s in range(4):
        ok = jnp.logical_and(fwd, sends_to[s])
        remote(ok, stored_faces[s], faces(V0)[s][1], device(1, s), R_V0 + s)
    remote(fwd, S0, interior(V0), partner, R_BULK)
    for s in range(4):
        src, dst = faces(Q)[s]
        remote(sends_to[s], src, dst, device(grp, s), R_P + s)

    @pl.when(fwd)
    def _():
        for c in fields_copies(V0, 3):
            c.wait()

    @pl.when(adj)
    def _():
        for c in fields_copies(L2, 3):
            c.wait()

    for s in range(4):
        src, dst = faces(V0)[s]
        remote(jnp.logical_and(fwd, sends_to[s]), src, dst, device(0, s), R_V0 + s)
        src, dst = faces(L2)[s]
        remote(jnp.logical_and(adj, sends_to[s]), src, dst, device(1, s), R_L2 + s)

    ld_own.wait()
    lane = lax.broadcasted_iota(jnp.int32, (1, 128), 1)
    quarter = lax.rem(lane, KT)
    ids = jnp.zeros((1, 128), jnp.int32)
    for k in range(KT):
        ids = jnp.where(quarter == k, OB[0:1, 128 * k : 128 * k + 128], ids)
    ocol[pl.ds(zz, 1), :] = ids
    ORow = ocol.at[pl.ds(zz, 1), :]

    def spread(src, dst, sem, rsm, peers):
        for dev in peers:
            pltpu.make_async_remote_copy(
                src_ref=src, dst_ref=dst, send_sem=sem, recv_sem=rsm,
                device_id=dev, device_id_type=MESH,
            ).start()

    spread(ORow, ORow, dsem.at[0], rsem.at[R_O1], [z_peer(d) for d in range(1, ZN)])

    for c in ld_heat:
        c.wait()

    arrive(adj, interior(V0), R_BULK)
    for s in range(4):
        arrive(has[s], faces(V0)[s][1], R_V0 + s)
        arrive(has[s], faces(Q)[s][1], R_P + s)

    lane4 = lax.broadcasted_iota(jnp.int32, (KT, 8, 128), 2)

    def z_next(x):
        r = pltpu.roll(x, 127, 2)
        after = jnp.concatenate([r[1:], jnp.zeros((1, 8, 128), F32)], axis=0)
        return jnp.where(lane4 == 127, after, r)

    def z_back(x, edge):
        r = pltpu.roll(x, 1, 2)
        before = jnp.concatenate([edge[None], r[:-1]], axis=0)
        return jnp.where(lane4 == 0, before, r)

    def conductivity(V):
        def row(i, _):
            KA[i] = 0.2 + Q[i] * (0.8 + 0.1 * V[i])
            return 0

        lax.fori_loop(0, CX + 2, row, 0)

    def at(ref, i, y):
        return ref[i, :, pl.ds(y, 8), :]

    def advance(V, put):
        conductivity(V)

        def body(i, _):
            for g in range(CY // 8):
                y = Y0 + 8 * g
                v, k = at(V, i, y), at(KA, i, y)
                flux = jnp.zeros_like(v)
                for di, dy in ((1, 0), (-1, 0), (0, 1), (0, -1)):
                    flux += (k + at(KA, i + di, y + dy)) * (at(V, i + di, y + dy) - v)
                up = (k + z_next(k)) * (z_next(v) - v)
                flux += up - z_back(up, k[0] * v[0])
                q = at(Q, i, y)
                h = HT[i - 1, :, pl.ds(8 * g, 8), :]
                put(i, g, v + 0.04 * (flux - v + q * v) + 0.08 * h)
            return 0

        lax.fori_loop(1, CX + 1, body, 0)

    def retreat(V, L, put):
        conductivity(V)

        def body(i, total):
            for g in range(CY // 8):
                y = Y0 + 8 * g
                v, k, l = at(V, i, y), at(KA, i, y), at(L, i, y)
                ss = jnp.zeros_like(v)
                tt = jnp.zeros_like(v)
                for di, dy in ((1, 0), (-1, 0), (0, 1), (0, -1)):
                    jump = l - at(L, i + di, y + dy)
                    ss += (at(V, i + di, y + dy) - v) * jump
                    tt += (k + at(KA, i + di, y + dy)) * jump
                jump = l - z_next(l)
                s = (z_next(v) - v) * jump
                t = (k + z_next(k)) * jump
                ss += s + z_back(s, -v[0] * l[0])
                tt += t - z_back(t, -k[0] * l[0])
                q = at(Q, i, y)
                new = l + 0.04 * (0.1 * q * ss - tt - l + q * l) + (v - S0[i - 1, :, pl.ds(8 * g, 8), :])
                porous = jnp.where(LB[i - 1, :, pl.ds(8 * g, 8), :] == 2, 0.04, 0.0)
                total = total + porous * ((0.8 + 0.1 * v) * ss + v * l)
                put(i, g, new)
            return total

        acc[...] += lax.fori_loop(1, CX + 1, body, jnp.zeros((KT, 8, 128), F32))

    def keep_in(ref):
        def put(i, g, x):
            ref[i, :, pl.ds(Y0 + 8 * g, 8), :] = x

        return put

    def keep_result(i, g, x):
        RES[i - 1, :, pl.ds(8 * g, 8), :] = x

    advance(V0, keep_in(V1))

    for s in range(4):
        src, dst = faces(V1)[s]
        remote(sends_to[s], src, dst, device(grp, s), R_V1 + s)

    pltpu.make_async_copy(ocol.at[pl.ds(0, ZN - 1)], ocol.at[pl.ds(0, ZN - 1)], rsem.at[R_O1]).wait()
    otab[cc] = ocol[...]
    spread(ocol, otab.at[cc], dsem.at[1], rsem.at[R_O2], [plane_peer(grp, d) for d in range(1, CN)])

    for s in range(4):
        arrive(has[s], faces(V1)[s][1], R_V1 + s)

    @pl.when(fwd)
    def _():
        advance(V1, keep_result)

    for s in range(4):
        arrive(jnp.logical_and(adj, has[s]), faces(L2)[s][1], R_L2 + s)

    @pl.when(adj)
    def _():
        acc[...] = jnp.zeros((KT, 8, 128), F32)
        retreat(V1, L2, keep_in(L1))

    for s in range(4):
        src, dst = faces(L1)[s]
        remote(jnp.logical_and(adj, sends_to[s]), src, dst, device(1, s), R_L1 + s)
    for s in range(4):
        arrive(jnp.logical_and(adj, has[s]), faces(L1)[s][1], R_L1 + s)

    @pl.when(adj)
    def _():
        retreat(V0, L1, keep_result)
        rows = jnp.sum(acc[...], axis=1, keepdims=True)
        lanes8 = lax.rem(lax.broadcasted_iota(jnp.int32, (8, 128), 1), KT)
        sums = jnp.zeros((8, 128), F32)
        for k in range(KT):
            x = jnp.broadcast_to(rows[k], (8, 128))
            total = x
            for i in range(KT):
                if i != k:
                    total = total + pltpu.roll(x, (k - i) % 128, 1)
            sums = jnp.where(lanes8 == k, total, sums)
        dcol[pl.ds(zz, 1), :] = sums[0:1]
        DRow = dcol.at[pl.ds(zz, 1), :]
        spread(DRow, DRow, dsem.at[2], rsem.at[R_D1], [z_peer(d) for d in range(1, ZN)])

    outs = [
        pltpu.make_async_copy(RES.at[:, k], out.at[0, :, :, pl.ds(128 * k, 128)], lsem.at[6, k])
        for k in range(KT)
    ]
    for c in outs:
        c.start()

    seven = pltpu.make_async_copy(dcol.at[pl.ds(0, ZN - 1)], dcol.at[pl.ds(0, ZN - 1)], rsem.at[R_D1])

    @pl.when(adj)
    def _():
        seven.wait()
        dtab[cc] = dcol[...]
        spread(
            dcol, dtab.at[cc], dsem.at[3], rsem.at[R_D2],
            [plane_peer(g, d) for d in range(1, CN) for g in (0, 1)] + [partner],
        )

    def tables(ref, n, sem):
        return pltpu.make_async_copy(ref.at[pl.ds(0, n)], ref.at[pl.ds(0, n)], sem)

    tables(otab, CN - 1, rsem.at[R_O2]).wait()

    @pl.when(fwd)
    def _():
        tables(dtab, CN, rsem.at[R_D2]).wait()

    @pl.when(adj)
    def _():
        tables(dtab, CN - 1, rsem.at[R_D2]).wait()

    base = (grp * NGX * NGY + gx * NGY + gy) * ND_DEV

    def pick(j, _):
        hit = otab[...] == base + j
        sel[pl.ds(j, 1), :] = jnp.sum(jnp.sum(jnp.where(hit, dtab[...], 0.0), axis=0), axis=0, keepdims=True)
        return 0

    lax.fori_loop(0, ND_DEV, pick, 0)
    each = jnp.sum(sel[...], axis=1, keepdims=True)
    row = lax.broadcasted_iota(jnp.int32, (ND_DEV, 128), 0)
    col = lax.broadcasted_iota(jnp.int32, (ND_DEV, 128), 1)
    sens[...] = jnp.sum(jnp.where(row == col, each, 0.0), axis=0, keepdims=True)

    for cond, make in sent:

        @pl.when(cond)
        def _():
            make().wait_send()

    pltpu.make_async_copy(ocol.at[pl.ds(0, ZN - 1)], ocol.at[pl.ds(0, ZN - 1)], dsem.at[0]).wait()
    tables(otab, CN - 1, dsem.at[1]).wait()

    @pl.when(adj)
    def _():
        pltpu.make_async_copy(dcol.at[pl.ds(0, ZN - 1)], dcol.at[pl.ds(0, ZN - 1)], dsem.at[2]).wait()
        tables(dtab, CN - 1, dsem.at[3]).wait()
        tables(dtab, CN, dsem.at[3]).wait()

    for c in outs:
        c.wait()


def shards(fields, stored, porosity, labels, heat_source, design_owner):
    anywhere = pl.BlockSpec(memory_space=pl.ANY)
    pad = pltpu.VMEM(PAD, F32)
    flat = pltpu.VMEM(FLAT, F32)
    out, sens = pl.pallas_call(
        kernel,
        out_shape=(
            jax.ShapeDtypeStruct((1, CX, CY, CZ), F32),
            jax.ShapeDtypeStruct((1, 128), F32),
        ),
        in_specs=[anywhere] * 6,
        out_specs=(anywhere, pl.BlockSpec(memory_space=pltpu.VMEM)),
        scratch_shapes=[
            pad, pad, pad, pad, pad, pad,
            flat, pltpu.VMEM(FLAT, jnp.int32), flat, flat, flat,
            pltpu.VMEM((8, CZ), jnp.int32),
            pltpu.VMEM((8, 128), jnp.int32), pltpu.VMEM((CN, 8, 128), jnp.int32),
            pltpu.VMEM((8, 128), F32), pltpu.VMEM((CN, 8, 128), F32),
            pltpu.VMEM((KT, 8, 128), F32), pltpu.VMEM((ND_DEV, 128), F32),
            pltpu.SemaphoreType.DMA((N_SEND,)),
            pltpu.SemaphoreType.DMA((N_RECV,)),
            pltpu.SemaphoreType.DMA((4,)),
            pltpu.SemaphoreType.DMA((7, KT)),
        ],
        compiler_params=pltpu.CompilerParams(collective_id=0, has_side_effects=True),
    )(fields, stored, porosity, labels, heat_source, design_owner)
    return out, sens[0, :ND_DEV]


def solution(mesh):
    return jax.shard_map(
        shards,
        mesh=mesh,
        in_specs=(
            P("grp", "gx", "gy", None),
            P("grp", "gx", "gy", None),
            P("gx", "gy", None),
            P("gx", "gy", None),
            P("gx", "gy", None),
            P("gx", "gy", None),
        ),
        out_specs=(P("grp", "gx", "gy", None), P(("grp", "gx", "gy"))),
        check_vma=False,
    )
```

```python
import jax
import jax.numpy as jnp
from jax import lax
from jax.experimental import pallas as pl
from jax.experimental.pallas import tpu as pltpu
from jax.sharding import PartitionSpec as P

MESH = pl.DeviceIdType.MESH
F32 = jnp.float32
YN, ZLN, ZHN, XN = 4, 4, 2, 4
NGX, NGY = YN * ZLN, ZHN * XN
ZN, CN = ZLN * ZHN, YN * XN
CX, CY, CZ = 8, 32, 512
KT = CZ // 128
Y0 = 8
YP = 48
PAD = (CX, KT, YP, 128)
FLAT = (CX, KT, CY, 128)
ND_DEV = 64
OUTSIDE = -0.25
ROWS = pl.ds(Y0, CY)
VIEWS = True

A_V0, A_Q, A_L2, A_V1, A_L1 = range(5)
R_BULK, R_O1, R_O2, R_D1, R_D2, R_QX, R_QY = range(20, 27)
N_RECV = 27
N_SEND = 48


def kernel(
    fields, stored, por, lab, heat, own,
    out, sens,
    V0, V1, KA, KB, KR, Q, L2, L1, RES, W0, WP, WM,
    S0, LB, PR, HT,
    HX, HY, FY, UX, UY,
    OB, ocol, otab, drow, dmix, dcol, dtab, acc, sel, rsel,
    ssem, rsem, dsem, lsem,
):
    grp = lax.axis_index("grp")
    gx = lax.axis_index("gx")
    gy = lax.axis_index("gy")
    fwd = grp == 0
    adj = grp == 1
    yy, zl = lax.div(gx, ZLN), lax.rem(gx, ZLN)
    zh, xx = lax.div(gy, XN), lax.rem(gy, XN)
    zz = zh * ZLN + zl
    cc = yy * XN + xx
    has = (gx > 0, gx < NGX - 1, gy > 0, gy < NGY - 1)
    sends_to = (has[1], has[0], has[3], has[2])

    def device(g, step):
        dx, dy = ((1, 0), (-1, 0), (0, 1), (0, -1))[step]
        return {"grp": g, "gx": lax.rem(gx + dx + NGX, NGX), "gy": lax.rem(gy + dy + NGY, NGY)}

    def column(g, y, x, z):
        return {"grp": g, "gx": y * ZLN + lax.rem(z, ZLN), "gy": lax.div(z, ZLN) * XN + x}

    def z_peer(d):
        return column(grp, yy, xx, lax.rem(zz + d, ZN))

    def plane_peer(g, d):
        c = lax.rem(cc + d, CN)
        return {"grp": g, "gx": lax.div(c, XN) * ZLN + zl, "gy": zh * XN + lax.rem(c, XN)}

    partner = {"grp": 1 - grp, "gx": gx, "gy": gy}
    y_up, y_down = lax.rem(yy + 1, YN), lax.rem(yy + YN - 1, YN)
    x_up, x_down = lax.rem(xx + 1, XN), lax.rem(xx + XN - 1, XN)

    bar = pltpu.get_barrier_semaphore()

    def tell(dev):
        pl.semaphore_signal(bar, inc=1, device_id=dev, device_id_type=MESH)

    for s in (2, 3, 0, 1):

        @pl.when(sends_to[s])
        def _():
            tell(device(grp, s))

        @pl.when(jnp.logical_and(adj, sends_to[s]))
        def _():
            tell(device(0, s))

    tell(partner)

    def load(src, dst, slot):
        copies = [
            pltpu.make_async_copy(src.at[:, :, pl.ds(128 * k, 128)], dst(k), lsem.at[slot, k])
            for k in range(KT)
        ]
        for c in copies:
            c.start()
        return copies

    ld_stored = load(stored.at[0], lambda k: S0.at[:, k], 0)
    ld_lab = load(lab, lambda k: LB.at[:, k], 1)
    ld_por = load(por, lambda k: PR.at[:, k], 2)

    def fields_copies(dst):
        return [
            pltpu.make_async_copy(
                fields.at[0, :, :, pl.ds(128 * k, 128)], dst.at[:, k, ROWS, :], lsem.at[3, k]
            )
            for k in range(KT)
        ]

    @pl.when(fwd)
    def _():
        for c in fields_copies(V0):
            c.start()

    @pl.when(adj)
    def _():
        for c in fields_copies(L2):
            c.start()

    ld_heat = load(heat, lambda k: HT.at[:, k], 4)
    ld_own = pltpu.make_async_copy(own.at[0, pl.ds(0, 8), :], OB, lsem.at[5, 0])
    ld_own.start()

    for d in range(1, ZN):
        tell(z_peer(d))
    for d in range(1, CN):
        tell(plane_peer(grp, d))

    @pl.when(fwd)
    def _():
        for d in range(1, CN):
            tell(plane_peer(1, d))

    @pl.when(adj)
    def _():
        for d in range(ZN):
            tell(column(1, yy, x_up, lax.rem(zz + d, ZN)))
            tell(column(1, yy, x_down, lax.rem(zz + d, ZN)))
        for h in range(ZHN):
            tell(column(1, y_down, xx, h * ZLN + ZLN - 1))
            tell(column(1, y_up, xx, h * ZLN))

    near = sum(h.astype(jnp.int32) for h in has)
    bottom, top = zl == 0, zl == ZLN - 1
    crossing = jnp.where(bottom, ZN, 0) + jnp.where(top, ZN, 0)
    told = ZN - 1 + CN - 1 + 1
    expected = jnp.where(fwd, 2 * near + told, near + told + CN - 1 + 2 * ZN + crossing)

    sub = lax.broadcasted_iota(jnp.int32, (KT, 8, 128), 1)
    lane4 = lax.broadcasted_iota(jnp.int32, (KT, 8, 128), 2)

    def z_next(x):
        r = pltpu.roll(x, 127, 2)
        after = jnp.concatenate([r[1:], jnp.zeros_like(r[:1])], axis=0)
        return jnp.where(lane4 == 127, after, r)

    def z_back(x, edge):
        r = pltpu.roll(x, 1, 2)
        before = jnp.concatenate([edge[None], r[:-1]], axis=0)
        return jnp.where(lane4 == 0, before, r)

    def at(ref, i, y):
        return ref[i, :, pl.ds(y, 8), :]

    def flat_at(ref, i, g):
        return ref[i, :, pl.ds(8 * g, 8), :]

    def around(ref, i, g, here):
        y = Y0 + 8 * g
        above, below = at(ref, i, y + 1), at(ref, i, y - 1)
        if g == CY // 8 - 1:
            above = jnp.where(sub == 7, here, above)
        if g == 0:
            below = jnp.where(sub == 0, here, below)
        return at(ref, jnp.minimum(i + 1, CX - 1), y), at(ref, jnp.maximum(i - 1, 0), y), above, below

    def sweep(body, init=0):
        return lax.fori_loop(0, CX, body, init)

    LAYER = (CX - 1, 0)
    ROW = (CY - 1, 0)
    SIDE_LAYER = (0, CX - 1)
    SIDE_ROW = (0, CY - 1)

    def get_lines(ref, row, pitch=YP, first=Y0):
        if not VIEWS:
            return jnp.stack([ref[:, k, first + row, :] for k in range(KT)], axis=0)
        flat = ref.reshape(CX * KT * pitch, 128)
        return jnp.stack(
            [flat[pl.ds(k * pitch + first + row, CX, stride=KT * pitch), :] for k in range(KT)], axis=0
        )

    def put_lines(ref, row, x, pitch=YP, first=Y0):
        for k in range(KT):
            if VIEWS:
                flat = ref.reshape(CX * KT * pitch, 128)
                flat[pl.ds(k * pitch + first + row, CX, stride=KT * pitch), :] = x[k]
            else:
                ref[:, k, first + row, :] = x[k]

    def layer(ref, i):
        return ref[i, :, ROWS, :]

    def conduct(q, v):
        return 0.2 + q * (0.8 + 0.1 * v)

    def conductivity(V, K):
        def body(i, _):
            K[i, :, ROWS, :] = conduct(Q[i, :, ROWS, :], V[i, :, ROWS, :])
            return 0

        sweep(body)

    for s in range(4):

        @pl.when(jnp.logical_not(has[s]))
        def _():
            for a in (A_V0, A_L2, A_V1, A_L1):
                if s < 2:
                    HX[a, s] = jnp.zeros((KT, CY, 128), F32)
                else:
                    HY[a, s - 2] = jnp.zeros((KT, CX, 128), F32)

        @pl.when(jnp.logical_and(adj, jnp.logical_not(has[s])))
        def _():
            if s < 2:
                HX[A_Q, s] = jnp.full((KT, CY, 128), OUTSIDE, F32)
            else:
                HY[A_Q, s - 2] = jnp.full((KT, CX, 128), OUTSIDE, F32)

    for c in ld_lab + ld_por:
        c.wait()

    def solid_share(i, _):
        label = LB[i]
        Q[i, :, ROWS, :] = jnp.where(label == 0, 1.0, jnp.where(label == 1, 0.0, PR[i]))
        return 0

    sweep(solid_share)
    for c in ld_stored:
        c.wait()
    for s in range(2):
        FY[A_Q, s] = get_lines(Q, ROW[s])

    @pl.when(fwd)
    def _():
        for s in range(2):
            FY[A_L2, s] = get_lines(S0, ROW[s], CY, 0)
        for c in fields_copies(V0):
            c.wait()
        for s in range(2):
            FY[A_V0, s] = get_lines(V0, ROW[s])

    @pl.when(adj)
    def _():
        for c in fields_copies(L2):
            c.wait()
        for s in range(2):
            FY[A_L2, s] = get_lines(L2, ROW[s])

    ld_own.wait()
    lane = lax.broadcasted_iota(jnp.int32, (1, 128), 1)
    quarter = lax.rem(lane, KT)
    ids = jnp.zeros((1, 128), jnp.int32)
    for k in range(KT):
        ids = jnp.where(quarter == k, OB[0:1, 128 * k : 128 * k + 128], ids)
    if ZN < 8:
        dcol[...] = jnp.zeros((8, 128), F32)
    ocol[pl.ds(zz, 1), :] = ids

    sent = []

    def remote(cond, src, dst, dev, recv):
        slot = len(sent)

        def make():
            return pltpu.make_async_remote_copy(
                src_ref=src, dst_ref=dst, send_sem=ssem.at[slot], recv_sem=rsem.at[recv],
                device_id=dev, device_id_type=MESH,
            )

        @pl.when(cond)
        def _():
            make().start()

        sent.append((cond, make))

    def arrive(cond, dst, recv):
        @pl.when(cond)
        def _():
            pltpu.make_async_copy(dst, dst, rsem.at[recv]).wait()

    def rim(a, s):
        return HX.at[a, s] if s < 2 else HY.at[a, s - 2]

    def send_faces(cond, g, a, layers, edge):
        for s in (2, 3, 0, 1):
            src = layers(LAYER[s]) if s < 2 else FY.at[edge, s - 2]
            remote(jnp.logical_and(cond, sends_to[s]), src, rim(a, s), device(g, s), 4 * a + s)

    def faces_arrive(cond, a):
        for s in range(4):
            arrive(jnp.logical_and(cond, has[s]), rim(a, s), 4 * a + s)

    def both(ref):
        return lambda i: ref.at[i, :, ROWS, :]

    pl.semaphore_wait(bar, expected)
    send_faces(fwd, 1, A_V0, lambda i: S0.at[i], A_L2)
    remote(fwd, S0, V0.at[:, :, ROWS, :], partner, R_BULK)
    send_faces(adj, 1, A_Q, both(Q), A_Q)
    send_faces(adj, 1, A_L2, both(L2), A_L2)
    send_faces(fwd, 0, A_V0, both(V0), A_V0)

    def spread(src, dst, sem, rsm, peers):
        for dev in peers:
            pltpu.make_async_remote_copy(
                src_ref=src, dst_ref=dst, send_sem=sem, recv_sem=rsm,
                device_id=dev, device_id_type=MESH,
            ).start()

    here = ocol.at[pl.ds(zz, 1), :]
    spread(here, here, dsem.at[0], rsem.at[R_O1], [z_peer(d) for d in range(1, ZN)])

    for c in ld_heat:
        c.wait()

    def advance(V, K, out_ref):
        def body(i, _):
            for g in range(CY // 8):
                y = Y0 + 8 * g
                v, k = at(V, i, y), at(K, i, y)
                flux = jnp.zeros_like(v)
                for vn, kn in zip(around(V, i, g, v), around(K, i, g, k)):
                    flux += (k + kn) * (vn - v)
                up = (k + z_next(k)) * (z_next(v) - v)
                flux += up - z_back(up, k[0] * v[0])
                q = at(Q, i, y)
                out_ref[i, :, pl.ds(y, 8), :] = v + 0.04 * (flux - v + q * v) + 0.08 * flat_at(HT, i, g)
            return 0

        sweep(body)

    def advance_rims(V, K, a, out_ref):
        for s in range(2):
            i = SIDE_LAYER[s]
            vn, qn = HX[a, s], HX[A_Q, s]
            flux = (layer(K, i) + conduct(qn, vn)) * (vn - layer(V, i))
            out_ref[i, :, ROWS, :] = layer(out_ref, i) + 0.04 * flux
        for s in range(2):
            j = SIDE_ROW[s]
            vn, qn, v = HY[a, s], HY[A_Q, s], get_lines(V, j)
            flux = (conduct(get_lines(Q, j), v) + conduct(qn, vn)) * (vn - v)
            put_lines(out_ref, j, get_lines(out_ref, j) + 0.04 * flux)

    def porous_at(i, g):
        return jnp.where(flat_at(LB, i, g) == 2, 0.04, 0.0)

    arrive(adj, V0.at[:, :, ROWS, :], R_BULK)
    conductivity(V0, KA)
    advance(V0, KA, V1)

    @pl.when(adj)
    def _():
        def rates(i, _):
            KR[i, :, ROWS, :] = jnp.where(LB[i] == 2, 0.04, 0.0) * (0.8 + 0.1 * V0[i, :, ROWS, :])
            return 0

        sweep(rates)

        def weights(i, _):
            for g in range(CY // 8):
                y = Y0 + 8 * g
                v, r = at(V0, i, y), at(KR, i, y)
                w = porous_at(i, g) * v
                for vn, rn in zip(around(V0, i, g, v), around(KR, i, g, r)):
                    w += (r + rn) * (vn - v)
                dz = z_next(v) - v
                W0[i, :, pl.ds(8 * g, 8), :] = w + r * (dz - z_back(dz, v[0]))
                WP[i, :, pl.ds(8 * g, 8), :] = -z_back(r * dz, jnp.zeros((8, 128), F32))
                WM[i, :, pl.ds(8 * g, 8), :] = z_next(r) * dz
            return 0

        sweep(weights)

    faces_arrive(adj, A_Q)
    remote(adj, HX.at[A_Q], HX.at[A_Q], partner, R_QX)
    remote(adj, HY.at[A_Q], HY.at[A_Q], partner, R_QY)
    arrive(fwd, HX.at[A_Q], R_QX)
    arrive(fwd, HY.at[A_Q], R_QY)
    faces_arrive(grp >= 0, A_V0)
    advance_rims(V0, KA, A_V0, V1)

    for s in range(2):
        FY[A_V1, s] = get_lines(V1, ROW[s])
    send_faces(grp >= 0, grp, A_V1, both(V1), A_V1)

    def rows_of(n, sem):
        return pltpu.make_async_copy(dmix.at[pl.ds(0, n)], dmix.at[pl.ds(0, n)], sem)

    rows_of(ZN - 1, rsem.at[R_O1]).wait()
    otab[cc] = ocol[...]
    spread(ocol, otab.at[cc], dsem.at[1], rsem.at[R_O2], [plane_peer(grp, d) for d in range(1, CN)])

    conductivity(V1, KB)

    @pl.when(fwd)
    def _():
        advance(V1, KB, RES)

    def retreat(V, K, L, out_ref, sums):
        def body(i, total):
            for g in range(CY // 8):
                y = Y0 + 8 * g
                v, k, l = at(V, i, y), at(K, i, y), at(L, i, y)
                ss = jnp.zeros_like(v)
                tt = jnp.zeros_like(v)
                for vn, kn, ln in zip(around(V, i, g, v), around(K, i, g, k), around(L, i, g, l)):
                    jump = l - ln
                    ss += (vn - v) * jump
                    tt += (k + kn) * jump
                jump = l - z_next(l)
                s = (z_next(v) - v) * jump
                t = (k + z_next(k)) * jump
                ss += s + z_back(s, -v[0] * l[0])
                tt += t - z_back(t, -k[0] * l[0])
                q = at(Q, i, y)
                out_ref[i, :, pl.ds(y, 8), :] = (
                    l + 0.04 * (0.1 * q * ss - tt - l + q * l) + (v - flat_at(S0, i, g))
                )
                if sums:
                    total = total + porous_at(i, g) * ((0.8 + 0.1 * v) * ss + v * l)
            return total

        return sweep(body, jnp.zeros((KT, 8, 128), F32))

    def retreat_rims(V, K, av, L, al, out_ref, sums):
        for s in range(2):
            i = SIDE_LAYER[s]
            v, l, vn = layer(V, i), layer(L, i), HX[av, s]
            jump = l - HX[al, s]
            ss = (vn - v) * jump
            tt = (layer(K, i) + conduct(HX[A_Q, s], vn)) * jump
            out_ref[i, :, ROWS, :] = layer(out_ref, i) + 0.04 * (0.1 * layer(Q, i) * ss - tt)
            if sums:
                x = jnp.where(LB[i] == 2, 0.04, 0.0) * (0.8 + 0.1 * v) * ss
                acc[0] += sum(x[:, 8 * g : 8 * g + 8] for g in range(CY // 8))
        for s in range(2):
            j = SIDE_ROW[s]
            v, l, q, vn = get_lines(V, j), get_lines(L, j), get_lines(Q, j), HY[av, s]
            jump = l - HY[al, s]
            ss = (vn - v) * jump
            tt = (conduct(q, v) + conduct(HY[A_Q, s], vn)) * jump
            put_lines(out_ref, j, get_lines(out_ref, j) + 0.04 * (0.1 * q * ss - tt))
            if sums:
                acc[0] += jnp.where(get_lines(LB, j, CY, 0) == 2, 0.04, 0.0) * (0.8 + 0.1 * v) * ss

    @pl.when(adj)
    def _():
        acc[0] = retreat(V1, KB, L2, L1, True)
        for s in range(2):
            i = SIDE_LAYER[s]
            v, vn, qn = layer(V0, i), HX[A_V0, s], HX[A_Q, s]
            W0[i] = W0[i] + layer(KR, i) * (vn - v)
            inside = jnp.logical_and(qn > 0.0, qn < 1.0)
            UX[s] = jnp.where(inside, 0.04, 0.0) * (0.8 + 0.1 * vn) * (vn - v)
        for s in range(2):
            j = SIDE_ROW[s]
            v, vn, qn = get_lines(V0, j), HY[A_V0, s], HY[A_Q, s]
            put_lines(W0, j, get_lines(W0, j, CY, 0) + get_lines(KR, j) * (vn - v), CY, 0)
            inside = jnp.logical_and(qn > 0.0, qn < 1.0)
            UY[s] = jnp.where(inside, 0.04, 0.0) * (0.8 + 0.1 * vn) * (vn - v)

    def tables(ref, n, sem):
        return pltpu.make_async_copy(ref.at[pl.ds(0, n)], ref.at[pl.ds(0, n)], sem)

    tables(otab, CN - 1, rsem.at[R_O2]).wait()
    base = (grp * NGX * NGY + gx * NGY + gy) * ND_DEV
    place = (
        lax.broadcasted_iota(jnp.int32, (CN, 8, 128), 0) * 8
        + lax.broadcasted_iota(jnp.int32, (CN, 8, 128), 1)
        + 1
    ).astype(F32)

    def find(j, _):
        hit = otab[...] == base + j
        rsel[pl.ds(j, 1), :] = jnp.sum(jnp.sum(jnp.where(hit, place, 0.0), axis=0), axis=0, keepdims=True)
        return 0

    lax.fori_loop(0, ND_DEV, find, 0)
    row_at = jnp.sum(rsel[...], axis=1, keepdims=True)
    spot = lax.broadcasted_iota(jnp.int32, (ND_DEV, CN * 8), 1).astype(F32)
    sel[...] = jnp.where(row_at == spot + 1.0, 1.0, 0.0)

    faces_arrive(grp >= 0, A_V1)

    @pl.when(fwd)
    def _():
        advance_rims(V1, KB, A_V1, RES)

    faces_arrive(adj, A_L2)

    @pl.when(adj)
    def _():
        retreat_rims(V1, KB, A_V1, L2, A_L2, L1, True)
        for s in range(2):
            FY[A_L1, s] = get_lines(L1, ROW[s])

        def weigh(i, totals):
            r0, rp, rm = totals
            for g in range(CY // 8):
                l = at(L1, i, Y0 + 8 * g)
                r0 = r0 + flat_at(W0, i, g) * l
                rp = rp + flat_at(WP, i, g) * l
                rm = rm + flat_at(WM, i, g) * l
            return r0, rp, rm

        zero = jnp.zeros((KT, 8, 128), F32)
        r0, rp, rm = sweep(weigh, (acc[0], zero, zero))
        own_sum = r0 + z_next(rp) + z_back(rm, jnp.zeros((8, 128), F32))
        parts = [own_sum]
        for s in (1, 0):
            x = UX[s] * layer(L1, SIDE_LAYER[s])
            parts.append(sum(x[:, 8 * g : 8 * g + 8] for g in range(CY // 8)))
        for s in (1, 0):
            parts.append(UY[s] * get_lines(L1, SIDE_ROW[s]))
        mixed = jnp.zeros((KT, 8, 128), F32)
        for n, x in enumerate(parts):
            mixed = jnp.where(sub == n, jnp.sum(x, axis=1, keepdims=True), mixed)
        lanes8 = lax.rem(lax.broadcasted_iota(jnp.int32, (8, 128), 1), KT)
        sums = jnp.zeros((8, 128), F32)
        for k in range(KT):
            x = mixed[k]
            total = x
            for i in range(KT):
                if i != k:
                    total = total + pltpu.roll(x, (k - i) % 128, 1)
            sums = jnp.where(lanes8 == k, total, sums)
        drow[...] = sums
        dmix[pl.ds(zz, 1), :] = drow[0:1]

        def scatter(kind, y, x, target, first):
            src, dst = drow.at[pl.ds(kind, 1), :], dmix.at[pl.ds(kind * ZN + target, 1), :]
            spread(
                src, dst, dsem.at[2], rsem.at[R_D1],
                [column(1, y, x, lax.rem(zz + d, ZN)) for d in range(first, ZN)],
            )

        z_up, z_down = lax.rem(zz + 1, ZN), lax.rem(zz + ZN - 1, ZN)
        flip = lax.rem(zz + ZLN * (ZHN - 1), ZN)
        lo_z, hi_z = zh * ZLN, zh * ZLN + ZLN - 1
        scatter(3, yy, x_up, jnp.where(xx == XN - 1, flip, zz), 0)
        scatter(4, yy, x_down, jnp.where(xx == 0, flip, zz), 0)
        scatter(0, yy, xx, zz, 1)
        y_to, z_to = jnp.where(top, y_up, yy), jnp.where(top, lo_z, z_up)
        scatter(1, y_to, xx, z_to, 1)
        y_from, z_from = jnp.where(bottom, y_down, yy), jnp.where(bottom, hi_z, z_down)
        scatter(2, y_from, xx, z_from, 1)

        def one(kind, y, target):
            pltpu.make_async_remote_copy(
                src_ref=drow.at[pl.ds(kind, 1), :], dst_ref=dmix.at[pl.ds(kind * ZN + target, 1), :],
                send_sem=dsem.at[2], recv_sem=rsem.at[R_D1],
                device_id=column(1, y, xx, zz), device_id_type=MESH,
            ).start()

        @pl.when(top)
        def _():
            one(1, y_up, lo_z)

        @pl.when(jnp.logical_not(top))
        def _():
            dmix[pl.ds(ZN + z_up, 1), :] = drow[1:2]

        @pl.when(bottom)
        def _():
            one(2, y_down, hi_z)

        @pl.when(jnp.logical_not(bottom))
        def _():
            dmix[pl.ds(2 * ZN + z_down, 1), :] = drow[2:3]

    send_faces(adj, 1, A_L1, both(L1), A_L1)

    def mixed_wait(sem):
        middle = jnp.logical_not(jnp.logical_or(bottom, top))

        @pl.when(middle)
        def _():
            rows_of(5 * ZN - 3, sem).wait()

        @pl.when(jnp.logical_not(middle))
        def _():
            rows_of(5 * ZN - 2, sem).wait()

    @pl.when(adj)
    def _():
        retreat(V0, KA, L1, RES, False)
        mixed_wait(rsem.at[R_D1])
        total = dmix[pl.ds(0, ZN), :]
        for n in range(1, 5):
            total = total + dmix[pl.ds(n * ZN, ZN), :]
        dcol[pl.ds(0, ZN), :] = total
        dtab[cc] = dcol[...]
        spread(
            dcol, dtab.at[cc], dsem.at[3], rsem.at[R_D2],
            [plane_peer(g, d) for d in range(1, CN) for g in (0, 1)] + [partner],
        )

    faces_arrive(adj, A_L1)

    @pl.when(adj)
    def _():
        retreat_rims(V0, KA, A_V0, L1, A_L1, RES, False)

    def result(i, _):
        for k in range(KT):
            out[0, i, :, 128 * k : 128 * k + 128] = RES[i, k, ROWS, :]
        return 0

    sweep(result)

    @pl.when(fwd)
    def _():
        tables(dtab, CN, rsem.at[R_D2]).wait()

    @pl.when(adj)
    def _():
        tables(dtab, CN - 1, rsem.at[R_D2]).wait()

    picked = jnp.dot(
        sel[...], dtab[...].reshape(CN * 8, 128), preferred_element_type=F32, precision=lax.Precision.HIGHEST
    )
    each = jnp.sum(jnp.where(rsel[...] > 0.0, picked, 0.0), axis=1, keepdims=True)
    row = lax.broadcasted_iota(jnp.int32, (ND_DEV, 128), 0)
    col = lax.broadcasted_iota(jnp.int32, (ND_DEV, 128), 1)
    sens[...] = jnp.sum(jnp.where(row == col, each, 0.0), axis=0, keepdims=True)

    for cond, make in sent:

        @pl.when(cond)
        def _():
            make().wait_send()

    rows_of(ZN - 1, dsem.at[0]).wait()
    tables(otab, CN - 1, dsem.at[1]).wait()

    @pl.when(adj)
    def _():
        mixed_wait(dsem.at[2])
        tables(dtab, CN - 1, dsem.at[3]).wait()
        tables(dtab, CN, dsem.at[3]).wait()


def shards(fields, stored, porosity, labels, heat_source, design_owner):
    anywhere = pl.BlockSpec(memory_space=pl.ANY)
    here = pl.BlockSpec(memory_space=pltpu.VMEM)
    pad = pltpu.VMEM(PAD, F32)
    flat = pltpu.VMEM(FLAT, F32)
    out, sens = pl.pallas_call(
        kernel,
        out_shape=(pltpu.VMEM((1, CX, CY, CZ), F32), pltpu.VMEM((1, 128), F32)),
        in_specs=[anywhere] * 6,
        out_specs=(here, here),
        scratch_shapes=[pad] * 9 + [flat] * 3 + [
            flat, pltpu.VMEM(FLAT, jnp.int32), flat, flat,
            pltpu.VMEM((5, 2, KT, CY, 128), F32), pltpu.VMEM((5, 2, KT, CX, 128), F32),
            pltpu.VMEM((5, 2, KT, CX, 128), F32),
            pltpu.VMEM((2, KT, CY, 128), F32), pltpu.VMEM((2, KT, CX, 128), F32),
            pltpu.VMEM((8, CZ), jnp.int32),
            pltpu.VMEM((8, 128), jnp.int32), pltpu.VMEM((CN, 8, 128), jnp.int32),
            pltpu.VMEM((8, 128), F32), pltpu.VMEM((5 * 8, 128), F32),
            pltpu.VMEM((8, 128), F32), pltpu.VMEM((CN, 8, 128), F32),
            pltpu.VMEM((1, KT, 8, 128), F32),
            pltpu.VMEM((ND_DEV, CN * 8), F32), pltpu.VMEM((ND_DEV, 128), F32),
            pltpu.SemaphoreType.DMA((N_SEND,)),
            pltpu.SemaphoreType.DMA((N_RECV,)),
            pltpu.SemaphoreType.DMA((4,)),
            pltpu.SemaphoreType.DMA((7, KT)),
        ],
        compiler_params=pltpu.CompilerParams(collective_id=0, has_side_effects=True),
    )(fields, stored, porosity, labels, heat_source, design_owner)
    return out, sens[0, :ND_DEV]


def solution(mesh):
    return jax.shard_map(
        shards,
        mesh=mesh,
        in_specs=(
            P("grp", "gx", "gy", None),
            P("grp", "gx", "gy", None),
            P("gx", "gy", None),
            P("gx", "gy", None),
            P("gx", "gy", None),
            P("gx", "gy", None),
        ),
        out_specs=(P("grp", "gx", "gy", None), P(("grp", "gx", "gy"))),
        check_vma=False,
    )
```

```python
import jax
import jax.numpy as jnp
from jax import lax
from jax.experimental import pallas as pl
from jax.experimental.pallas import tpu as pltpu
from jax.sharding import PartitionSpec as P

MESH = pl.DeviceIdType.MESH
F32 = jnp.float32
YN, ZLN, ZHN, XN = 4, 4, 2, 4
NGX, NGY = YN * ZLN, ZHN * XN
ZN, CN = ZLN * ZHN, YN * XN
CX, CY, CZ = 8, 32, 512
KT = CZ // 128
Y0 = 8
YP = 48
PAD = (CX, KT, YP, 128)
FLAT = (CX, KT, CY, 128)
ND_DEV = 64
OUTSIDE = -0.25
ROWS = pl.ds(Y0, CY)
VIEWS = True

Z_STEPS = sorted(range(1, ZN), key=lambda d: -min(d, ZN - d))
PLANE_STEPS = sorted(
    ((dy, dx) for dy in range(YN) for dx in range(XN) if dy or dx),
    key=lambda o: -min(o[0], YN - o[0]) - min(o[1], XN - o[1]),
)

A_V0, A_Q, A_L2, A_V1, A_L1 = range(5)
R_BULK, R_O1, R_O2, R_D1, R_D2, R_QX, R_QY = range(20, 27)
N_RECV = 27
N_SEND = 48


def kernel(
    fields, stored, por, lab, heat, own,
    out, sens,
    V0, V1, KA, KB, KR, Q, L2, L1, RES, W0, WP, WM,
    S0, LB, PR, HT,
    HX, HY, FY, UX, UY,
    OB, ocol, otab, drow, dmix, dcol, dtab, acc, sel, rsel,
    ssem, rsem, dsem, lsem,
):
    grp = lax.axis_index("grp")
    gx = lax.axis_index("gx")
    gy = lax.axis_index("gy")
    fwd = grp == 0
    adj = grp == 1
    yy, zl = lax.div(gx, ZLN), lax.rem(gx, ZLN)
    zh, xx = lax.div(gy, XN), lax.rem(gy, XN)
    zz = zh * ZLN + zl
    cc = yy * XN + xx
    has = (gx > 0, gx < NGX - 1, gy > 0, gy < NGY - 1)
    sends_to = (has[1], has[0], has[3], has[2])

    def device(g, step):
        dx, dy = ((1, 0), (-1, 0), (0, 1), (0, -1))[step]
        return {"grp": g, "gx": lax.rem(gx + dx + NGX, NGX), "gy": lax.rem(gy + dy + NGY, NGY)}

    def column(g, y, x, z):
        return {"grp": g, "gx": y * ZLN + lax.rem(z, ZLN), "gy": lax.div(z, ZLN) * XN + x}

    def z_peer(d):
        return column(grp, yy, xx, lax.rem(zz + d, ZN))

    def plane_peer(g, o):
        return {"grp": g, "gx": lax.rem(yy + o[0], YN) * ZLN + zl, "gy": zh * XN + lax.rem(xx + o[1], XN)}

    partner = {"grp": 1 - grp, "gx": gx, "gy": gy}
    y_up, y_down = lax.rem(yy + 1, YN), lax.rem(yy + YN - 1, YN)
    x_up, x_down = lax.rem(xx + 1, XN), lax.rem(xx + XN - 1, XN)

    bar = pltpu.get_barrier_semaphore()

    def tell(dev):
        pl.semaphore_signal(bar, inc=1, device_id=dev, device_id_type=MESH)

    for s in (2, 3, 0, 1):

        @pl.when(sends_to[s])
        def _():
            tell(device(grp, s))

        @pl.when(jnp.logical_and(adj, sends_to[s]))
        def _():
            tell(device(0, s))

    tell(partner)

    def load(src, dst, slot):
        copies = [
            pltpu.make_async_copy(src.at[:, :, pl.ds(128 * k, 128)], dst(k), lsem.at[slot, k])
            for k in range(KT)
        ]
        for c in copies:
            c.start()
        return copies

    ld_stored = load(stored.at[0], lambda k: S0.at[:, k], 0)
    ld_lab = load(lab, lambda k: LB.at[:, k], 1)
    ld_por = load(por, lambda k: PR.at[:, k], 2)

    def fields_copies(dst):
        return [
            pltpu.make_async_copy(
                fields.at[0, :, :, pl.ds(128 * k, 128)], dst.at[:, k, ROWS, :], lsem.at[3, k]
            )
            for k in range(KT)
        ]

    @pl.when(fwd)
    def _():
        for c in fields_copies(V0):
            c.start()

    @pl.when(adj)
    def _():
        for c in fields_copies(L2):
            c.start()

    ld_heat = load(heat, lambda k: HT.at[:, k], 4)
    ld_own = pltpu.make_async_copy(own.at[0, pl.ds(0, 8), :], OB, lsem.at[5, 0])
    ld_own.start()

    for d in Z_STEPS:
        tell(z_peer(d))
    for o in PLANE_STEPS:
        tell(plane_peer(grp, o))

    @pl.when(fwd)
    def _():
        for o in PLANE_STEPS:
            tell(plane_peer(1, o))

    @pl.when(adj)
    def _():
        for d in range(ZN):
            tell(column(1, yy, x_up, lax.rem(zz + d, ZN)))
            tell(column(1, yy, x_down, lax.rem(zz + d, ZN)))
        for h in range(ZHN):
            tell(column(1, y_down, xx, h * ZLN + ZLN - 1))
            tell(column(1, y_up, xx, h * ZLN))

    near = sum(h.astype(jnp.int32) for h in has)
    bottom, top = zl == 0, zl == ZLN - 1
    crossing = jnp.where(bottom, ZN, 0) + jnp.where(top, ZN, 0)
    told = ZN - 1 + CN - 1 + 1
    expected = jnp.where(fwd, 2 * near + told, near + told + CN - 1 + 2 * ZN + crossing)

    sub = lax.broadcasted_iota(jnp.int32, (KT, 8, 128), 1)
    lane4 = lax.broadcasted_iota(jnp.int32, (KT, 8, 128), 2)

    def z_next(x):
        r = pltpu.roll(x, 127, 2)
        after = jnp.concatenate([r[1:], jnp.zeros_like(r[:1])], axis=0)
        return jnp.where(lane4 == 127, after, r)

    def z_back(x, edge):
        r = pltpu.roll(x, 1, 2)
        before = jnp.concatenate([edge[None], r[:-1]], axis=0)
        return jnp.where(lane4 == 0, before, r)

    def at(ref, i, y):
        return ref[i, :, pl.ds(y, 8), :]

    def flat_at(ref, i, g):
        return ref[i, :, pl.ds(8 * g, 8), :]

    def around(ref, i, g, here):
        y = Y0 + 8 * g
        above, below = at(ref, i, y + 1), at(ref, i, y - 1)
        if g == CY // 8 - 1:
            above = jnp.where(sub == 7, here, above)
        if g == 0:
            below = jnp.where(sub == 0, here, below)
        return at(ref, jnp.minimum(i + 1, CX - 1), y), at(ref, jnp.maximum(i - 1, 0), y), above, below

    def sweep(body, init=0):
        return lax.fori_loop(0, CX, body, init)

    LAYER = (CX - 1, 0)
    ROW = (CY - 1, 0)
    SIDE_LAYER = (0, CX - 1)
    SIDE_ROW = (0, CY - 1)

    def get_lines(ref, row, pitch=YP, first=Y0):
        if not VIEWS:
            return jnp.stack([ref[:, k, first + row, :] for k in range(KT)], axis=0)
        flat = ref.reshape(CX * KT * pitch, 128)
        return jnp.stack(
            [flat[pl.ds(k * pitch + first + row, CX, stride=KT * pitch), :] for k in range(KT)], axis=0
        )

    def put_lines(ref, row, x, pitch=YP, first=Y0):
        for k in range(KT):
            if VIEWS:
                flat = ref.reshape(CX * KT * pitch, 128)
                flat[pl.ds(k * pitch + first + row, CX, stride=KT * pitch), :] = x[k]
            else:
                ref[:, k, first + row, :] = x[k]

    def layer(ref, i):
        return ref[i, :, ROWS, :]

    def conduct(q, v):
        return 0.2 + q * (0.8 + 0.1 * v)

    def conductivity(V, K):
        def body(i, _):
            K[i, :, ROWS, :] = conduct(Q[i, :, ROWS, :], V[i, :, ROWS, :])
            return 0

        sweep(body)

    for s in range(4):

        @pl.when(jnp.logical_not(has[s]))
        def _():
            for a in (A_V0, A_L2, A_V1, A_L1):
                if s < 2:
                    HX[a, s] = jnp.zeros((KT, CY, 128), F32)
                else:
                    HY[a, s - 2] = jnp.zeros((KT, CX, 128), F32)

        @pl.when(jnp.logical_and(adj, jnp.logical_not(has[s])))
        def _():
            if s < 2:
                HX[A_Q, s] = jnp.full((KT, CY, 128), OUTSIDE, F32)
            else:
                HY[A_Q, s - 2] = jnp.full((KT, CX, 128), OUTSIDE, F32)

    for c in ld_lab + ld_por:
        c.wait()

    def solid_share(i, _):
        label = LB[i]
        Q[i, :, ROWS, :] = jnp.where(label == 0, 1.0, jnp.where(label == 1, 0.0, PR[i]))
        return 0

    sweep(solid_share)
    for c in ld_stored:
        c.wait()
    for s in range(2):
        FY[A_Q, s] = get_lines(Q, ROW[s])

    @pl.when(fwd)
    def _():
        for s in range(2):
            FY[A_L2, s] = get_lines(S0, ROW[s], CY, 0)
        for c in fields_copies(V0):
            c.wait()
        for s in range(2):
            FY[A_V0, s] = get_lines(V0, ROW[s])

    @pl.when(adj)
    def _():
        for c in fields_copies(L2):
            c.wait()
        for s in range(2):
            FY[A_L2, s] = get_lines(L2, ROW[s])

    ld_own.wait()
    lane = lax.broadcasted_iota(jnp.int32, (1, 128), 1)
    quarter = lax.rem(lane, KT)
    ids = jnp.zeros((1, 128), jnp.int32)
    for k in range(KT):
        ids = jnp.where(quarter == k, OB[0:1, 128 * k : 128 * k + 128], ids)
    if ZN < 8:
        dcol[...] = jnp.zeros((8, 128), F32)
    ocol[pl.ds(zz, 1), :] = ids

    sent = []

    def remote(cond, src, dst, dev, recv):
        slot = len(sent)

        def make():
            return pltpu.make_async_remote_copy(
                src_ref=src, dst_ref=dst, send_sem=ssem.at[slot], recv_sem=rsem.at[recv],
                device_id=dev, device_id_type=MESH,
            )

        @pl.when(cond)
        def _():
            make().start()

        sent.append((cond, make))

    def arrive(cond, dst, recv):
        @pl.when(cond)
        def _():
            pltpu.make_async_copy(dst, dst, rsem.at[recv]).wait()

    def rim(a, s):
        return HX.at[a, s] if s < 2 else HY.at[a, s - 2]

    def send_faces(cond, g, a, layers, edge):
        for s in (2, 3, 0, 1):
            src = layers(LAYER[s]) if s < 2 else FY.at[edge, s - 2]
            remote(jnp.logical_and(cond, sends_to[s]), src, rim(a, s), device(g, s), 4 * a + s)

    def faces_arrive(cond, a):
        for s in range(4):
            arrive(jnp.logical_and(cond, has[s]), rim(a, s), 4 * a + s)

    def both(ref):
        return lambda i: ref.at[i, :, ROWS, :]

    pl.semaphore_wait(bar, expected)
    send_faces(fwd, 1, A_V0, lambda i: S0.at[i], A_L2)
    remote(fwd, S0, V0.at[:, :, ROWS, :], partner, R_BULK)
    send_faces(adj, 1, A_Q, both(Q), A_Q)

    def spread(src, dst, sem, rsm, peers):
        for dev in peers:
            pltpu.make_async_remote_copy(
                src_ref=src, dst_ref=dst, send_sem=sem, recv_sem=rsm,
                device_id=dev, device_id_type=MESH,
            ).start()

    here = ocol.at[pl.ds(zz, 1), :]
    spread(here, here, dsem.at[0], rsem.at[R_O1], [z_peer(d) for d in Z_STEPS])

    for c in ld_heat:
        c.wait()

    def advance(V, K, out_ref):
        def body(i, _):
            for g in range(CY // 8):
                y = Y0 + 8 * g
                v, k = at(V, i, y), at(K, i, y)
                flux = jnp.zeros_like(v)
                for vn, kn in zip(around(V, i, g, v), around(K, i, g, k)):
                    flux += (k + kn) * (vn - v)
                up = (k + z_next(k)) * (z_next(v) - v)
                flux += up - z_back(up, k[0] * v[0])
                q = at(Q, i, y)
                out_ref[i, :, pl.ds(y, 8), :] = v + 0.04 * (flux - v + q * v) + 0.08 * flat_at(HT, i, g)
            return 0

        sweep(body)

    def advance_rims(V, K, a, out_ref):
        for s in range(2):
            i = SIDE_LAYER[s]
            vn, qn = HX[a, s], HX[A_Q, s]
            flux = (layer(K, i) + conduct(qn, vn)) * (vn - layer(V, i))
            out_ref[i, :, ROWS, :] = layer(out_ref, i) + 0.04 * flux
        for s in range(2):
            j = SIDE_ROW[s]
            vn, qn, v = HY[a, s], HY[A_Q, s], get_lines(V, j)
            flux = (conduct(get_lines(Q, j), v) + conduct(qn, vn)) * (vn - v)
            put_lines(out_ref, j, get_lines(out_ref, j) + 0.04 * flux)

    def porous_at(i, g):
        return jnp.where(flat_at(LB, i, g) == 2, 0.04, 0.0)

    arrive(adj, V0.at[:, :, ROWS, :], R_BULK)
    conductivity(V0, KA)
    advance(V0, KA, V1)
    send_faces(adj, 1, A_L2, both(L2), A_L2)
    send_faces(fwd, 0, A_V0, both(V0), A_V0)

    @pl.when(adj)
    def _():
        def rates(i, _):
            KR[i, :, ROWS, :] = jnp.where(LB[i] == 2, 0.04, 0.0) * (0.8 + 0.1 * V0[i, :, ROWS, :])
            return 0

        sweep(rates)

        def weights(i, _):
            for g in range(CY // 8):
                y = Y0 + 8 * g
                v, r = at(V0, i, y), at(KR, i, y)
                w = porous_at(i, g) * v
                for vn, rn in zip(around(V0, i, g, v), around(KR, i, g, r)):
                    w += (r + rn) * (vn - v)
                dz = z_next(v) - v
                W0[i, :, pl.ds(8 * g, 8), :] = w + r * (dz - z_back(dz, v[0]))
                WP[i, :, pl.ds(8 * g, 8), :] = -z_back(r * dz, jnp.zeros((8, 128), F32))
                WM[i, :, pl.ds(8 * g, 8), :] = z_next(r) * dz
            return 0

        sweep(weights)

    faces_arrive(adj, A_Q)
    remote(adj, HX.at[A_Q], HX.at[A_Q], partner, R_QX)
    remote(adj, HY.at[A_Q], HY.at[A_Q], partner, R_QY)
    arrive(fwd, HX.at[A_Q], R_QX)
    arrive(fwd, HY.at[A_Q], R_QY)
    faces_arrive(grp >= 0, A_V0)
    advance_rims(V0, KA, A_V0, V1)

    for s in range(2):
        FY[A_V1, s] = get_lines(V1, ROW[s])
    send_faces(grp >= 0, grp, A_V1, both(V1), A_V1)

    def rows_of(n, sem):
        return pltpu.make_async_copy(dmix.at[pl.ds(0, n)], dmix.at[pl.ds(0, n)], sem)

    rows_of(ZN - 1, rsem.at[R_O1]).wait()
    otab[cc] = ocol[...]
    spread(ocol, otab.at[cc], dsem.at[1], rsem.at[R_O2], [plane_peer(grp, o) for o in PLANE_STEPS])

    conductivity(V1, KB)

    @pl.when(fwd)
    def _():
        advance(V1, KB, RES)

    def retreat(V, K, L, out_ref, sums):
        def body(i, total):
            for g in range(CY // 8):
                y = Y0 + 8 * g
                v, k, l = at(V, i, y), at(K, i, y), at(L, i, y)
                ss = jnp.zeros_like(v)
                tt = jnp.zeros_like(v)
                for vn, kn, ln in zip(around(V, i, g, v), around(K, i, g, k), around(L, i, g, l)):
                    jump = l - ln
                    ss += (vn - v) * jump
                    tt += (k + kn) * jump
                jump = l - z_next(l)
                s = (z_next(v) - v) * jump
                t = (k + z_next(k)) * jump
                ss += s + z_back(s, -v[0] * l[0])
                tt += t - z_back(t, -k[0] * l[0])
                q = at(Q, i, y)
                out_ref[i, :, pl.ds(y, 8), :] = (
                    l + 0.04 * (0.1 * q * ss - tt - l + q * l) + (v - flat_at(S0, i, g))
                )
                if sums:
                    total = total + porous_at(i, g) * ((0.8 + 0.1 * v) * ss + v * l)
            return total

        return sweep(body, jnp.zeros((KT, 8, 128), F32))

    def retreat_rims(V, K, av, L, al, out_ref, sums):
        for s in range(2):
            i = SIDE_LAYER[s]
            v, l, vn = layer(V, i), layer(L, i), HX[av, s]
            jump = l - HX[al, s]
            ss = (vn - v) * jump
            tt = (layer(K, i) + conduct(HX[A_Q, s], vn)) * jump
            out_ref[i, :, ROWS, :] = layer(out_ref, i) + 0.04 * (0.1 * layer(Q, i) * ss - tt)
            if sums:
                x = jnp.where(LB[i] == 2, 0.04, 0.0) * (0.8 + 0.1 * v) * ss
                acc[0] += sum(x[:, 8 * g : 8 * g + 8] for g in range(CY // 8))
        for s in range(2):
            j = SIDE_ROW[s]
            v, l, q, vn = get_lines(V, j), get_lines(L, j), get_lines(Q, j), HY[av, s]
            jump = l - HY[al, s]
            ss = (vn - v) * jump
            tt = (conduct(q, v) + conduct(HY[A_Q, s], vn)) * jump
            put_lines(out_ref, j, get_lines(out_ref, j) + 0.04 * (0.1 * q * ss - tt))
            if sums:
                acc[0] += jnp.where(get_lines(LB, j, CY, 0) == 2, 0.04, 0.0) * (0.8 + 0.1 * v) * ss

    @pl.when(adj)
    def _():
        acc[0] = retreat(V1, KB, L2, L1, True)
        for s in range(2):
            i = SIDE_LAYER[s]
            v, vn, qn = layer(V0, i), HX[A_V0, s], HX[A_Q, s]
            W0[i] = W0[i] + layer(KR, i) * (vn - v)
            inside = jnp.logical_and(qn > 0.0, qn < 1.0)
            UX[s] = jnp.where(inside, 0.04, 0.0) * (0.8 + 0.1 * vn) * (vn - v)
        for s in range(2):
            j = SIDE_ROW[s]
            v, vn, qn = get_lines(V0, j), HY[A_V0, s], HY[A_Q, s]
            put_lines(W0, j, get_lines(W0, j, CY, 0) + get_lines(KR, j) * (vn - v), CY, 0)
            inside = jnp.logical_and(qn > 0.0, qn < 1.0)
            UY[s] = jnp.where(inside, 0.04, 0.0) * (0.8 + 0.1 * vn) * (vn - v)

    faces_arrive(grp >= 0, A_V1)

    @pl.when(fwd)
    def _():
        advance_rims(V1, KB, A_V1, RES)

    faces_arrive(adj, A_L2)

    @pl.when(adj)
    def _():
        retreat_rims(V1, KB, A_V1, L2, A_L2, L1, True)
        for s in range(2):
            FY[A_L1, s] = get_lines(L1, ROW[s])

        def weigh(i, totals):
            r0, rp, rm = totals
            for g in range(CY // 8):
                l = at(L1, i, Y0 + 8 * g)
                r0 = r0 + flat_at(W0, i, g) * l
                rp = rp + flat_at(WP, i, g) * l
                rm = rm + flat_at(WM, i, g) * l
            return r0, rp, rm

        zero = jnp.zeros((KT, 8, 128), F32)
        r0, rp, rm = sweep(weigh, (acc[0], zero, zero))
        own_sum = r0 + z_next(rp) + z_back(rm, jnp.zeros((8, 128), F32))
        parts = [own_sum]
        for s in (1, 0):
            x = UX[s] * layer(L1, SIDE_LAYER[s])
            parts.append(sum(x[:, 8 * g : 8 * g + 8] for g in range(CY // 8)))
        for s in (1, 0):
            parts.append(UY[s] * get_lines(L1, SIDE_ROW[s]))
        mixed = jnp.zeros((KT, 8, 128), F32)
        for n, x in enumerate(parts):
            mixed = jnp.where(sub == n, jnp.sum(x, axis=1, keepdims=True), mixed)
        lanes8 = lax.rem(lax.broadcasted_iota(jnp.int32, (8, 128), 1), KT)
        sums = jnp.zeros((8, 128), F32)
        for k in range(KT):
            x = mixed[k]
            total = x
            for i in range(KT):
                if i != k:
                    total = total + pltpu.roll(x, (k - i) % 128, 1)
            sums = jnp.where(lanes8 == k, total, sums)
        drow[...] = sums
        dmix[pl.ds(zz, 1), :] = drow[0:1]

        def scatter(kind, y, x, target, first):
            src, dst = drow.at[pl.ds(kind, 1), :], dmix.at[pl.ds(kind * ZN + target, 1), :]
            spread(
                src, dst, dsem.at[2], rsem.at[R_D1],
                [column(1, y, x, lax.rem(zz + d, ZN)) for d in Z_STEPS + [0] * (1 - first)],
            )

        z_up, z_down = lax.rem(zz + 1, ZN), lax.rem(zz + ZN - 1, ZN)
        flip = lax.rem(zz + ZLN * (ZHN - 1), ZN)
        lo_z, hi_z = zh * ZLN, zh * ZLN + ZLN - 1
        scatter(3, yy, x_up, jnp.where(xx == XN - 1, flip, zz), 0)
        scatter(4, yy, x_down, jnp.where(xx == 0, flip, zz), 0)
        scatter(0, yy, xx, zz, 1)
        y_to, z_to = jnp.where(top, y_up, yy), jnp.where(top, lo_z, z_up)
        scatter(1, y_to, xx, z_to, 1)
        y_from, z_from = jnp.where(bottom, y_down, yy), jnp.where(bottom, hi_z, z_down)
        scatter(2, y_from, xx, z_from, 1)

        def one(kind, y, target):
            pltpu.make_async_remote_copy(
                src_ref=drow.at[pl.ds(kind, 1), :], dst_ref=dmix.at[pl.ds(kind * ZN + target, 1), :],
                send_sem=dsem.at[2], recv_sem=rsem.at[R_D1],
                device_id=column(1, y, xx, zz), device_id_type=MESH,
            ).start()

        @pl.when(top)
        def _():
            one(1, y_up, lo_z)

        @pl.when(jnp.logical_not(top))
        def _():
            dmix[pl.ds(ZN + z_up, 1), :] = drow[1:2]

        @pl.when(bottom)
        def _():
            one(2, y_down, hi_z)

        @pl.when(jnp.logical_not(bottom))
        def _():
            dmix[pl.ds(2 * ZN + z_down, 1), :] = drow[2:3]

    send_faces(adj, 1, A_L1, both(L1), A_L1)

    def mixed_wait(sem):
        middle = jnp.logical_not(jnp.logical_or(bottom, top))

        @pl.when(middle)
        def _():
            rows_of(5 * ZN - 3, sem).wait()

        @pl.when(jnp.logical_not(middle))
        def _():
            rows_of(5 * ZN - 2, sem).wait()

    @pl.when(adj)
    def _():
        retreat(V0, KA, L1, RES, False)

    def tables(ref, n, sem):
        return pltpu.make_async_copy(ref.at[pl.ds(0, n)], ref.at[pl.ds(0, n)], sem)

    tables(otab, CN - 1, rsem.at[R_O2]).wait()
    base = (grp * NGX * NGY + gx * NGY + gy) * ND_DEV
    place = (
        lax.broadcasted_iota(jnp.int32, (CN, 8, 128), 0) * 8
        + lax.broadcasted_iota(jnp.int32, (CN, 8, 128), 1)
        + 1
    ).astype(F32)

    def find(j, _):
        hit = otab[...] == base + j
        rsel[pl.ds(j, 1), :] = jnp.sum(jnp.sum(jnp.where(hit, place, 0.0), axis=0), axis=0, keepdims=True)
        return 0

    lax.fori_loop(0, ND_DEV, find, 0)
    row_at = jnp.sum(rsel[...], axis=1, keepdims=True)
    spot = lax.broadcasted_iota(jnp.int32, (ND_DEV, CN * 8), 1).astype(F32)
    sel[...] = jnp.where(row_at == spot + 1.0, 1.0, 0.0)

    @pl.when(adj)
    def _():
        mixed_wait(rsem.at[R_D1])
        total = dmix[pl.ds(0, ZN), :]
        for n in range(1, 5):
            total = total + dmix[pl.ds(n * ZN, ZN), :]
        dcol[pl.ds(0, ZN), :] = total
        dtab[cc] = dcol[...]
        spread(
            dcol, dtab.at[cc], dsem.at[3], rsem.at[R_D2],
            [plane_peer(g, o) for o in PLANE_STEPS for g in (1, 0)] + [partner],
        )

    faces_arrive(adj, A_L1)

    @pl.when(adj)
    def _():
        retreat_rims(V0, KA, A_V0, L1, A_L1, RES, False)

    def result(i, _):
        for k in range(KT):
            out[0, i, :, 128 * k : 128 * k + 128] = RES[i, k, ROWS, :]
        return 0

    sweep(result)

    @pl.when(fwd)
    def _():
        tables(dtab, CN, rsem.at[R_D2]).wait()

    @pl.when(adj)
    def _():
        tables(dtab, CN - 1, rsem.at[R_D2]).wait()

    picked = jnp.dot(
        sel[...], dtab[...].reshape(CN * 8, 128), preferred_element_type=F32, precision=lax.Precision.HIGHEST
    )
    each = jnp.sum(jnp.where(rsel[...] > 0.0, picked, 0.0), axis=1, keepdims=True)
    row = lax.broadcasted_iota(jnp.int32, (ND_DEV, 128), 0)
    col = lax.broadcasted_iota(jnp.int32, (ND_DEV, 128), 1)
    sens[...] = jnp.sum(jnp.where(row == col, each, 0.0), axis=0, keepdims=True)

    for cond, make in sent:

        @pl.when(cond)
        def _():
            make().wait_send()

    rows_of(ZN - 1, dsem.at[0]).wait()
    tables(otab, CN - 1, dsem.at[1]).wait()

    @pl.when(adj)
    def _():
        mixed_wait(dsem.at[2])
        tables(dtab, CN - 1, dsem.at[3]).wait()
        tables(dtab, CN, dsem.at[3]).wait()


def shards(fields, stored, porosity, labels, heat_source, design_owner):
    anywhere = pl.BlockSpec(memory_space=pl.ANY)
    here = pl.BlockSpec(memory_space=pltpu.VMEM)
    pad = pltpu.VMEM(PAD, F32)
    flat = pltpu.VMEM(FLAT, F32)
    out, sens = pl.pallas_call(
        kernel,
        out_shape=(pltpu.VMEM((1, CX, CY, CZ), F32), pltpu.VMEM((1, 128), F32)),
        in_specs=[anywhere] * 6,
        out_specs=(here, here),
        scratch_shapes=[pad] * 9 + [flat] * 3 + [
            flat, pltpu.VMEM(FLAT, jnp.int32), flat, flat,
            pltpu.VMEM((5, 2, KT, CY, 128), F32), pltpu.VMEM((5, 2, KT, CX, 128), F32),
            pltpu.VMEM((5, 2, KT, CX, 128), F32),
            pltpu.VMEM((2, KT, CY, 128), F32), pltpu.VMEM((2, KT, CX, 128), F32),
            pltpu.VMEM((8, CZ), jnp.int32),
            pltpu.VMEM((8, 128), jnp.int32), pltpu.VMEM((CN, 8, 128), jnp.int32),
            pltpu.VMEM((8, 128), F32), pltpu.VMEM((5 * 8, 128), F32),
            pltpu.VMEM((8, 128), F32), pltpu.VMEM((CN, 8, 128), F32),
            pltpu.VMEM((1, KT, 8, 128), F32),
            pltpu.VMEM((ND_DEV, CN * 8), F32), pltpu.VMEM((ND_DEV, 128), F32),
            pltpu.SemaphoreType.DMA((N_SEND,)),
            pltpu.SemaphoreType.DMA((N_RECV,)),
            pltpu.SemaphoreType.DMA((4,)),
            pltpu.SemaphoreType.DMA((7, KT)),
        ],
        compiler_params=pltpu.CompilerParams(collective_id=0, has_side_effects=True),
    )(fields, stored, porosity, labels, heat_source, design_owner)
    return out, sens[0, :ND_DEV]


def solution(mesh):
    return jax.shard_map(
        shards,
        mesh=mesh,
        in_specs=(
            P("grp", "gx", "gy", None),
            P("grp", "gx", "gy", None),
            P("gx", "gy", None),
            P("gx", "gy", None),
            P("gx", "gy", None),
            P("gx", "gy", None),
        ),
        out_specs=(P("grp", "gx", "gy", None), P(("grp", "gx", "gy"))),
        check_vma=False,
    )
```

```python
import jax
import jax.numpy as jnp
from jax import lax
from jax.experimental import pallas as pl
from jax.experimental.pallas import tpu as pltpu
from jax.sharding import PartitionSpec as P

MESH = pl.DeviceIdType.MESH
F32 = jnp.float32
YN, ZLN, ZHN, XN = 4, 4, 2, 4
NGX, NGY = YN * ZLN, ZHN * XN
ZN, CN = ZLN * ZHN, YN * XN
CX, CY, CZ = 8, 32, 512
KT = CZ // 128
Y0 = 8
YP = 48
PAD = (CX, KT, YP, 128)
FLAT = (CX, KT, CY, 128)
ND_DEV = 64
OUTSIDE = -0.25
ROWS = pl.ds(Y0, CY)
VIEWS = True

Z_STEPS = sorted(range(1, ZN), key=lambda d: -min(d, ZN - d))
PLANE_STEPS = sorted(
    ((dy, dx) for dy in range(YN) for dx in range(XN) if dy or dx),
    key=lambda o: -min(o[0], YN - o[0]) - min(o[1], XN - o[1]),
)

A_V0, A_Q, A_L2, A_V1, A_L1 = range(5)
R_BULK, R_O1, R_O2, R_D1, R_D2, R_QX, R_QY = range(20, 27)
N_RECV = 27
N_SEND = 48


def kernel(
    fields, stored, por, lab, heat, own,
    out, sens,
    V0, V1, KA, KB, KR, Q, L2, L1, RES, W0, WP, WM,
    S0, LB, PR, HT,
    HX, HY, FY, UX, UY,
    OB, ocol, otab, drow, dmix, dcol, dtab, acc, sel, rsel,
    ssem, rsem, dsem, lsem, ready,
):
    grp = lax.axis_index("grp")
    gx = lax.axis_index("gx")
    gy = lax.axis_index("gy")
    fwd = grp == 0
    adj = grp == 1
    yy, zl = lax.div(gx, ZLN), lax.rem(gx, ZLN)
    zh, xx = lax.div(gy, XN), lax.rem(gy, XN)
    zz = zh * ZLN + zl
    cc = yy * XN + xx
    has = (gx > 0, gx < NGX - 1, gy > 0, gy < NGY - 1)
    sends_to = (has[1], has[0], has[3], has[2])

    def device(g, step):
        dx, dy = ((1, 0), (-1, 0), (0, 1), (0, -1))[step]
        return {"grp": g, "gx": lax.rem(gx + dx + NGX, NGX), "gy": lax.rem(gy + dy + NGY, NGY)}

    def column(g, y, x, z):
        return {"grp": g, "gx": y * ZLN + lax.rem(z, ZLN), "gy": lax.div(z, ZLN) * XN + x}

    def z_peer(d):
        return column(grp, yy, xx, lax.rem(zz + d, ZN))

    def plane_peer(g, o):
        return {"grp": g, "gx": lax.rem(yy + o[0], YN) * ZLN + zl, "gy": zh * XN + lax.rem(xx + o[1], XN)}

    partner = {"grp": 1 - grp, "gx": gx, "gy": gy}
    y_up, y_down = lax.rem(yy + 1, YN), lax.rem(yy + YN - 1, YN)
    x_up, x_down = lax.rem(xx + 1, XN), lax.rem(xx + XN - 1, XN)

    bar = pltpu.get_barrier_semaphore()

    def tell(dev):
        pl.semaphore_signal(bar, inc=1, device_id=dev, device_id_type=MESH)

    for s in (2, 3, 0, 1):

        @pl.when(sends_to[s])
        def _():
            tell(device(grp, s))

        @pl.when(jnp.logical_and(adj, sends_to[s]))
        def _():
            tell(device(0, s))

    tell(partner)

    def load(src, dst, slot):
        copies = [
            pltpu.make_async_copy(src.at[:, :, pl.ds(128 * k, 128)], dst(k), lsem.at[slot, k])
            for k in range(KT)
        ]
        for c in copies:
            c.start()
        return copies

    ld_stored = load(stored.at[0], lambda k: S0.at[:, k], 0)
    ld_lab = load(lab, lambda k: LB.at[:, k], 1)
    ld_por = load(por, lambda k: PR.at[:, k], 2)

    def fields_copies(dst):
        return [
            pltpu.make_async_copy(
                fields.at[0, :, :, pl.ds(128 * k, 128)], dst.at[:, k, ROWS, :], lsem.at[3, k]
            )
            for k in range(KT)
        ]

    @pl.when(fwd)
    def _():
        for c in fields_copies(V0):
            c.start()

    @pl.when(adj)
    def _():
        for c in fields_copies(L2):
            c.start()

    ld_heat = load(heat, lambda k: HT.at[:, k], 4)
    ld_own = pltpu.make_async_copy(own.at[0, pl.ds(0, 8), :], OB, lsem.at[5, 0])
    ld_own.start()

    for d in Z_STEPS:
        tell(z_peer(d))
    for o in PLANE_STEPS:
        tell(plane_peer(grp, o))

    @pl.when(fwd)
    def _():
        for o in PLANE_STEPS:
            tell(plane_peer(1, o))

    near = sum(h.astype(jnp.int32) for h in has)
    bottom, top = zl == 0, zl == ZLN - 1
    told = ZN - 1 + CN - 1 + 1
    expected = jnp.where(fwd, 2 * near + told, near + told + CN - 1)

    sub = lax.broadcasted_iota(jnp.int32, (KT, 8, 128), 1)
    lane4 = lax.broadcasted_iota(jnp.int32, (KT, 8, 128), 2)

    def z_next(x):
        r = pltpu.roll(x, 127, 2)
        after = jnp.concatenate([r[1:], jnp.zeros_like(r[:1])], axis=0)
        return jnp.where(lane4 == 127, after, r)

    def z_back(x, edge):
        r = pltpu.roll(x, 1, 2)
        before = jnp.concatenate([edge[None], r[:-1]], axis=0)
        return jnp.where(lane4 == 0, before, r)

    def at(ref, i, y):
        return ref[i, :, pl.ds(y, 8), :]

    def flat_at(ref, i, g):
        return ref[i, :, pl.ds(8 * g, 8), :]

    def around(ref, i, g, here):
        y = Y0 + 8 * g
        above, below = at(ref, i, y + 1), at(ref, i, y - 1)
        if g == CY // 8 - 1:
            above = jnp.where(sub == 7, here, above)
        if g == 0:
            below = jnp.where(sub == 0, here, below)
        return at(ref, jnp.minimum(i + 1, CX - 1), y), at(ref, jnp.maximum(i - 1, 0), y), above, below

    def sweep(body, init=0):
        return lax.fori_loop(0, CX, body, init)

    LAYER = (CX - 1, 0)
    ROW = (CY - 1, 0)
    SIDE_LAYER = (0, CX - 1)
    SIDE_ROW = (0, CY - 1)

    def get_lines(ref, row, pitch=YP, first=Y0):
        if not VIEWS:
            return jnp.stack([ref[:, k, first + row, :] for k in range(KT)], axis=0)
        flat = ref.reshape(CX * KT * pitch, 128)
        return jnp.stack(
            [flat[pl.ds(k * pitch + first + row, CX, stride=KT * pitch), :] for k in range(KT)], axis=0
        )

    def put_lines(ref, row, x, pitch=YP, first=Y0):
        for k in range(KT):
            if VIEWS:
                flat = ref.reshape(CX * KT * pitch, 128)
                flat[pl.ds(k * pitch + first + row, CX, stride=KT * pitch), :] = x[k]
            else:
                ref[:, k, first + row, :] = x[k]

    def layer(ref, i):
        return ref[i, :, ROWS, :]

    def conduct(q, v):
        return 0.2 + q * (0.8 + 0.1 * v)

    def conductivity(V, K):
        def body(i, _):
            K[i, :, ROWS, :] = conduct(Q[i, :, ROWS, :], V[i, :, ROWS, :])
            return 0

        sweep(body)

    for s in range(4):

        @pl.when(jnp.logical_not(has[s]))
        def _():
            for a in (A_V0, A_L2, A_V1, A_L1):
                if s < 2:
                    HX[a, s] = jnp.zeros((KT, CY, 128), F32)
                else:
                    HY[a, s - 2] = jnp.zeros((KT, CX, 128), F32)

        @pl.when(jnp.logical_and(adj, jnp.logical_not(has[s])))
        def _():
            if s < 2:
                HX[A_Q, s] = jnp.full((KT, CY, 128), OUTSIDE, F32)
            else:
                HY[A_Q, s - 2] = jnp.full((KT, CX, 128), OUTSIDE, F32)

    for c in ld_lab + ld_por:
        c.wait()

    def solid_share(i, _):
        label = LB[i]
        Q[i, :, ROWS, :] = jnp.where(label == 0, 1.0, jnp.where(label == 1, 0.0, PR[i]))
        return 0

    sweep(solid_share)
    for c in ld_stored:
        c.wait()
    for s in range(2):
        FY[A_Q, s] = get_lines(Q, ROW[s])

    @pl.when(fwd)
    def _():
        for s in range(2):
            FY[A_L2, s] = get_lines(S0, ROW[s], CY, 0)
        for c in fields_copies(V0):
            c.wait()
        for s in range(2):
            FY[A_V0, s] = get_lines(V0, ROW[s])

    @pl.when(adj)
    def _():
        for c in fields_copies(L2):
            c.wait()
        for s in range(2):
            FY[A_L2, s] = get_lines(L2, ROW[s])

    ld_own.wait()
    lane = lax.broadcasted_iota(jnp.int32, (1, 128), 1)
    quarter = lax.rem(lane, KT)
    ids = jnp.zeros((1, 128), jnp.int32)
    for k in range(KT):
        ids = jnp.where(quarter == k, OB[0:1, 128 * k : 128 * k + 128], ids)
    if ZN < 8:
        dcol[...] = jnp.zeros((8, 128), F32)
    ocol[pl.ds(zz, 1), :] = ids

    sent = []

    def remote(cond, src, dst, dev, recv):
        slot = len(sent)

        def make():
            return pltpu.make_async_remote_copy(
                src_ref=src, dst_ref=dst, send_sem=ssem.at[slot], recv_sem=rsem.at[recv],
                device_id=dev, device_id_type=MESH,
            )

        @pl.when(cond)
        def _():
            make().start()

        sent.append((cond, make))

    def arrive(cond, dst, recv):
        @pl.when(cond)
        def _():
            pltpu.make_async_copy(dst, dst, rsem.at[recv]).wait()

    def rim(a, s):
        return HX.at[a, s] if s < 2 else HY.at[a, s - 2]

    def send_faces(cond, g, a, layers, edge):
        for s in (2, 3, 0, 1):
            src = layers(LAYER[s]) if s < 2 else FY.at[edge, s - 2]
            remote(jnp.logical_and(cond, sends_to[s]), src, rim(a, s), device(g, s), 4 * a + s)

    def faces_arrive(cond, a):
        for s in range(4):
            arrive(jnp.logical_and(cond, has[s]), rim(a, s), 4 * a + s)

    def both(ref):
        return lambda i: ref.at[i, :, ROWS, :]

    pl.semaphore_wait(bar, expected)
    send_faces(fwd, 1, A_V0, lambda i: S0.at[i], A_L2)
    remote(fwd, S0, V0.at[:, :, ROWS, :], partner, R_BULK)
    send_faces(adj, 1, A_Q, both(Q), A_Q)

    def spread(src, dst, sem, rsm, peers):
        for dev in peers:
            pltpu.make_async_remote_copy(
                src_ref=src, dst_ref=dst, send_sem=sem, recv_sem=rsm,
                device_id=dev, device_id_type=MESH,
            ).start()

    @pl.when(adj)
    def _():
        for o in ((0, 1), (0, XN - 1), (1, 0), (YN - 1, 0)):
            pl.semaphore_signal(ready, inc=1, device_id=plane_peer(1, o), device_id_type=MESH)

    here = ocol.at[pl.ds(zz, 1), :]
    spread(here, here, dsem.at[0], rsem.at[R_O1], [z_peer(d) for d in Z_STEPS])

    for c in ld_heat:
        c.wait()

    def advance(V, K, out_ref):
        def body(i, _):
            for g in range(CY // 8):
                y = Y0 + 8 * g
                v, k = at(V, i, y), at(K, i, y)
                flux = jnp.zeros_like(v)
                for vn, kn in zip(around(V, i, g, v), around(K, i, g, k)):
                    flux += (k + kn) * (vn - v)
                up = (k + z_next(k)) * (z_next(v) - v)
                flux += up - z_back(up, k[0] * v[0])
                q = at(Q, i, y)
                out_ref[i, :, pl.ds(y, 8), :] = v + 0.04 * (flux - v + q * v) + 0.08 * flat_at(HT, i, g)
            return 0

        sweep(body)

    def advance_rims(V, K, a, out_ref):
        for s in range(2):
            i = SIDE_LAYER[s]
            vn, qn = HX[a, s], HX[A_Q, s]
            flux = (layer(K, i) + conduct(qn, vn)) * (vn - layer(V, i))
            out_ref[i, :, ROWS, :] = layer(out_ref, i) + 0.04 * flux
        for s in range(2):
            j = SIDE_ROW[s]
            vn, qn, v = HY[a, s], HY[A_Q, s], get_lines(V, j)
            flux = (conduct(get_lines(Q, j), v) + conduct(qn, vn)) * (vn - v)
            put_lines(out_ref, j, get_lines(out_ref, j) + 0.04 * flux)

    def porous_at(i, g):
        return jnp.where(flat_at(LB, i, g) == 2, 0.04, 0.0)

    arrive(adj, V0.at[:, :, ROWS, :], R_BULK)
    conductivity(V0, KA)
    advance(V0, KA, V1)
    send_faces(adj, 1, A_L2, both(L2), A_L2)
    send_faces(fwd, 0, A_V0, both(V0), A_V0)

    @pl.when(adj)
    def _():
        def rates(i, _):
            KR[i, :, ROWS, :] = jnp.where(LB[i] == 2, 0.04, 0.0) * (0.8 + 0.1 * V0[i, :, ROWS, :])
            return 0

        sweep(rates)

        def weights(i, _):
            for g in range(CY // 8):
                y = Y0 + 8 * g
                v, r = at(V0, i, y), at(KR, i, y)
                w = porous_at(i, g) * v
                for vn, rn in zip(around(V0, i, g, v), around(KR, i, g, r)):
                    w += (r + rn) * (vn - v)
                dz = z_next(v) - v
                W0[i, :, pl.ds(8 * g, 8), :] = w + r * (dz - z_back(dz, v[0]))
                WP[i, :, pl.ds(8 * g, 8), :] = -z_back(r * dz, jnp.zeros((8, 128), F32))
                WM[i, :, pl.ds(8 * g, 8), :] = z_next(r) * dz
            return 0

        sweep(weights)

    faces_arrive(adj, A_Q)
    remote(adj, HX.at[A_Q], HX.at[A_Q], partner, R_QX)
    remote(adj, HY.at[A_Q], HY.at[A_Q], partner, R_QY)
    arrive(fwd, HX.at[A_Q], R_QX)
    arrive(fwd, HY.at[A_Q], R_QY)
    faces_arrive(grp >= 0, A_V0)
    advance_rims(V0, KA, A_V0, V1)

    for s in range(2):
        FY[A_V1, s] = get_lines(V1, ROW[s])
    send_faces(grp >= 0, grp, A_V1, both(V1), A_V1)

    def rows_of(n, sem):
        return pltpu.make_async_copy(dmix.at[pl.ds(0, n)], dmix.at[pl.ds(0, n)], sem)

    rows_of(ZN - 1, rsem.at[R_O1]).wait()
    otab[cc] = ocol[...]
    spread(ocol, otab.at[cc], dsem.at[1], rsem.at[R_O2], [plane_peer(grp, o) for o in PLANE_STEPS])

    conductivity(V1, KB)

    @pl.when(fwd)
    def _():
        advance(V1, KB, RES)

    def retreat(V, K, L, out_ref, sums):
        def body(i, total):
            for g in range(CY // 8):
                y = Y0 + 8 * g
                v, k, l = at(V, i, y), at(K, i, y), at(L, i, y)
                ss = jnp.zeros_like(v)
                tt = jnp.zeros_like(v)
                for vn, kn, ln in zip(around(V, i, g, v), around(K, i, g, k), around(L, i, g, l)):
                    jump = l - ln
                    ss += (vn - v) * jump
                    tt += (k + kn) * jump
                jump = l - z_next(l)
                s = (z_next(v) - v) * jump
                t = (k + z_next(k)) * jump
                ss += s + z_back(s, -v[0] * l[0])
                tt += t - z_back(t, -k[0] * l[0])
                q = at(Q, i, y)
                out_ref[i, :, pl.ds(y, 8), :] = (
                    l + 0.04 * (0.1 * q * ss - tt - l + q * l) + (v - flat_at(S0, i, g))
                )
                if sums:
                    total = total + porous_at(i, g) * ((0.8 + 0.1 * v) * ss + v * l)
            return total

        return sweep(body, jnp.zeros((KT, 8, 128), F32))

    def retreat_rims(V, K, av, L, al, out_ref, sums):
        for s in range(2):
            i = SIDE_LAYER[s]
            v, l, vn = layer(V, i), layer(L, i), HX[av, s]
            jump = l - HX[al, s]
            ss = (vn - v) * jump
            tt = (layer(K, i) + conduct(HX[A_Q, s], vn)) * jump
            out_ref[i, :, ROWS, :] = layer(out_ref, i) + 0.04 * (0.1 * layer(Q, i) * ss - tt)
            if sums:
                x = jnp.where(LB[i] == 2, 0.04, 0.0) * (0.8 + 0.1 * v) * ss
                acc[0] += sum(x[:, 8 * g : 8 * g + 8] for g in range(CY // 8))
        for s in range(2):
            j = SIDE_ROW[s]
            v, l, q, vn = get_lines(V, j), get_lines(L, j), get_lines(Q, j), HY[av, s]
            jump = l - HY[al, s]
            ss = (vn - v) * jump
            tt = (conduct(q, v) + conduct(HY[A_Q, s], vn)) * jump
            put_lines(out_ref, j, get_lines(out_ref, j) + 0.04 * (0.1 * q * ss - tt))
            if sums:
                acc[0] += jnp.where(get_lines(LB, j, CY, 0) == 2, 0.04, 0.0) * (0.8 + 0.1 * v) * ss

    @pl.when(adj)
    def _():
        acc[0] = retreat(V1, KB, L2, L1, True)
        for s in range(2):
            i = SIDE_LAYER[s]
            v, vn, qn = layer(V0, i), HX[A_V0, s], HX[A_Q, s]
            W0[i] = W0[i] + layer(KR, i) * (vn - v)
            inside = jnp.logical_and(qn > 0.0, qn < 1.0)
            UX[s] = jnp.where(inside, 0.04, 0.0) * (0.8 + 0.1 * vn) * (vn - v)
        for s in range(2):
            j = SIDE_ROW[s]
            v, vn, qn = get_lines(V0, j), HY[A_V0, s], HY[A_Q, s]
            put_lines(W0, j, get_lines(W0, j, CY, 0) + get_lines(KR, j) * (vn - v), CY, 0)
            inside = jnp.logical_and(qn > 0.0, qn < 1.0)
            UY[s] = jnp.where(inside, 0.04, 0.0) * (0.8 + 0.1 * vn) * (vn - v)

    faces_arrive(grp >= 0, A_V1)

    @pl.when(fwd)
    def _():
        advance_rims(V1, KB, A_V1, RES)

    faces_arrive(adj, A_L2)

    @pl.when(adj)
    def _():
        retreat_rims(V1, KB, A_V1, L2, A_L2, L1, True)
        for s in range(2):
            FY[A_L1, s] = get_lines(L1, ROW[s])

        def weigh(i, totals):
            r0, rp, rm = totals
            for g in range(CY // 8):
                l = at(L1, i, Y0 + 8 * g)
                r0 = r0 + flat_at(W0, i, g) * l
                rp = rp + flat_at(WP, i, g) * l
                rm = rm + flat_at(WM, i, g) * l
            return r0, rp, rm

        zero = jnp.zeros((KT, 8, 128), F32)
        r0, rp, rm = sweep(weigh, (acc[0], zero, zero))
        own_sum = r0 + z_next(rp) + z_back(rm, jnp.zeros((8, 128), F32))
        parts = [own_sum]
        for s in (1, 0):
            x = UX[s] * layer(L1, SIDE_LAYER[s])
            parts.append(sum(x[:, 8 * g : 8 * g + 8] for g in range(CY // 8)))
        for s in (1, 0):
            parts.append(UY[s] * get_lines(L1, SIDE_ROW[s]))
        mixed = jnp.zeros((KT, 8, 128), F32)
        for n, x in enumerate(parts):
            mixed = jnp.where(sub == n, jnp.sum(x, axis=1, keepdims=True), mixed)
        lanes8 = lax.rem(lax.broadcasted_iota(jnp.int32, (8, 128), 1), KT)
        sums = jnp.zeros((8, 128), F32)
        for k in range(KT):
            x = mixed[k]
            total = x
            for i in range(KT):
                if i != k:
                    total = total + pltpu.roll(x, (k - i) % 128, 1)
            sums = jnp.where(lanes8 == k, total, sums)
        drow[...] = sums
        dmix[pl.ds(zz, 1), :] = drow[0:1]

        def scatter(kind, y, x, target, first):
            src, dst = drow.at[pl.ds(kind, 1), :], dmix.at[pl.ds(kind * ZN + target, 1), :]
            spread(
                src, dst, dsem.at[2], rsem.at[R_D1],
                [column(1, y, x, lax.rem(zz + d, ZN)) for d in Z_STEPS + [0] * (1 - first)],
            )

        pl.semaphore_wait(ready, 4)
        z_up, z_down = lax.rem(zz + 1, ZN), lax.rem(zz + ZN - 1, ZN)
        flip = lax.rem(zz + ZLN * (ZHN - 1), ZN)
        lo_z, hi_z = zh * ZLN, zh * ZLN + ZLN - 1
        scatter(3, yy, x_up, jnp.where(xx == XN - 1, flip, zz), 0)
        scatter(4, yy, x_down, jnp.where(xx == 0, flip, zz), 0)
        scatter(0, yy, xx, zz, 1)
        y_to, z_to = jnp.where(top, y_up, yy), jnp.where(top, lo_z, z_up)
        scatter(1, y_to, xx, z_to, 1)
        y_from, z_from = jnp.where(bottom, y_down, yy), jnp.where(bottom, hi_z, z_down)
        scatter(2, y_from, xx, z_from, 1)

        def one(kind, y, target):
            pltpu.make_async_remote_copy(
                src_ref=drow.at[pl.ds(kind, 1), :], dst_ref=dmix.at[pl.ds(kind * ZN + target, 1), :],
                send_sem=dsem.at[2], recv_sem=rsem.at[R_D1],
                device_id=column(1, y, xx, zz), device_id_type=MESH,
            ).start()

        @pl.when(top)
        def _():
            one(1, y_up, lo_z)

        @pl.when(jnp.logical_not(top))
        def _():
            dmix[pl.ds(ZN + z_up, 1), :] = drow[1:2]

        @pl.when(bottom)
        def _():
            one(2, y_down, hi_z)

        @pl.when(jnp.logical_not(bottom))
        def _():
            dmix[pl.ds(2 * ZN + z_down, 1), :] = drow[2:3]

    send_faces(adj, 1, A_L1, both(L1), A_L1)

    def mixed_wait(sem):
        middle = jnp.logical_not(jnp.logical_or(bottom, top))

        @pl.when(middle)
        def _():
            rows_of(5 * ZN - 3, sem).wait()

        @pl.when(jnp.logical_not(middle))
        def _():
            rows_of(5 * ZN - 2, sem).wait()

    @pl.when(adj)
    def _():
        retreat(V0, KA, L1, RES, False)

    def tables(ref, n, sem):
        return pltpu.make_async_copy(ref.at[pl.ds(0, n)], ref.at[pl.ds(0, n)], sem)

    tables(otab, CN - 1, rsem.at[R_O2]).wait()
    base = (grp * NGX * NGY + gx * NGY + gy) * ND_DEV
    place = (
        lax.broadcasted_iota(jnp.int32, (CN, 8, 128), 0) * 8
        + lax.broadcasted_iota(jnp.int32, (CN, 8, 128), 1)
        + 1
    ).astype(F32)

    def find(j, _):
        hit = otab[...] == base + j
        rsel[pl.ds(j, 1), :] = jnp.sum(jnp.sum(jnp.where(hit, place, 0.0), axis=0), axis=0, keepdims=True)
        return 0

    lax.fori_loop(0, ND_DEV, find, 0)
    row_at = jnp.sum(rsel[...], axis=1, keepdims=True)
    spot = lax.broadcasted_iota(jnp.int32, (ND_DEV, CN * 8), 1).astype(F32)
    sel[...] = jnp.where(row_at == spot + 1.0, 1.0, 0.0)

    @pl.when(adj)
    def _():
        mixed_wait(rsem.at[R_D1])
        total = dmix[pl.ds(0, ZN), :]
        for n in range(1, 5):
            total = total + dmix[pl.ds(n * ZN, ZN), :]
        dcol[pl.ds(0, ZN), :] = total
        dtab[cc] = dcol[...]
        spread(
            dcol, dtab.at[cc], dsem.at[3], rsem.at[R_D2],
            [plane_peer(g, o) for o in PLANE_STEPS for g in (1, 0)] + [partner],
        )

    faces_arrive(adj, A_L1)

    @pl.when(adj)
    def _():
        retreat_rims(V0, KA, A_V0, L1, A_L1, RES, False)

    def result(i, _):
        for k in range(KT):
            out[0, i, :, 128 * k : 128 * k + 128] = RES[i, k, ROWS, :]
        return 0

    sweep(result)

    @pl.when(fwd)
    def _():
        tables(dtab, CN, rsem.at[R_D2]).wait()

    @pl.when(adj)
    def _():
        tables(dtab, CN - 1, rsem.at[R_D2]).wait()

    picked = jnp.dot(
        sel[...], dtab[...].reshape(CN * 8, 128), preferred_element_type=F32, precision=lax.Precision.HIGHEST
    )
    each = jnp.sum(jnp.where(rsel[...] > 0.0, picked, 0.0), axis=1, keepdims=True)
    row = lax.broadcasted_iota(jnp.int32, (ND_DEV, 128), 0)
    col = lax.broadcasted_iota(jnp.int32, (ND_DEV, 128), 1)
    sens[...] = jnp.sum(jnp.where(row == col, each, 0.0), axis=0, keepdims=True)

    for cond, make in sent:

        @pl.when(cond)
        def _():
            make().wait_send()

    rows_of(ZN - 1, dsem.at[0]).wait()
    tables(otab, CN - 1, dsem.at[1]).wait()

    @pl.when(adj)
    def _():
        mixed_wait(dsem.at[2])
        tables(dtab, CN - 1, dsem.at[3]).wait()
        tables(dtab, CN, dsem.at[3]).wait()


def shards(fields, stored, porosity, labels, heat_source, design_owner):
    anywhere = pl.BlockSpec(memory_space=pl.ANY)
    here = pl.BlockSpec(memory_space=pltpu.VMEM)
    pad = pltpu.VMEM(PAD, F32)
    flat = pltpu.VMEM(FLAT, F32)
    out, sens = pl.pallas_call(
        kernel,
        out_shape=(pltpu.VMEM((1, CX, CY, CZ), F32), pltpu.VMEM((1, 128), F32)),
        in_specs=[anywhere] * 6,
        out_specs=(here, here),
        scratch_shapes=[pad] * 9 + [flat] * 3 + [
            flat, pltpu.VMEM(FLAT, jnp.int32), flat, flat,
            pltpu.VMEM((5, 2, KT, CY, 128), F32), pltpu.VMEM((5, 2, KT, CX, 128), F32),
            pltpu.VMEM((5, 2, KT, CX, 128), F32),
            pltpu.VMEM((2, KT, CY, 128), F32), pltpu.VMEM((2, KT, CX, 128), F32),
            pltpu.VMEM((8, CZ), jnp.int32),
            pltpu.VMEM((8, 128), jnp.int32), pltpu.VMEM((CN, 8, 128), jnp.int32),
            pltpu.VMEM((8, 128), F32), pltpu.VMEM((5 * 8, 128), F32),
            pltpu.VMEM((8, 128), F32), pltpu.VMEM((CN, 8, 128), F32),
            pltpu.VMEM((1, KT, 8, 128), F32),
            pltpu.VMEM((ND_DEV, CN * 8), F32), pltpu.VMEM((ND_DEV, 128), F32),
            pltpu.SemaphoreType.DMA((N_SEND,)),
            pltpu.SemaphoreType.DMA((N_RECV,)),
            pltpu.SemaphoreType.DMA((4,)),
            pltpu.SemaphoreType.DMA((7, KT)),
            pltpu.SemaphoreType.REGULAR,
        ],
        compiler_params=pltpu.CompilerParams(collective_id=0, has_side_effects=True),
    )(fields, stored, porosity, labels, heat_source, design_owner)
    return out, sens[0, :ND_DEV]


def solution(mesh):
    return jax.shard_map(
        shards,
        mesh=mesh,
        in_specs=(
            P("grp", "gx", "gy", None),
            P("grp", "gx", "gy", None),
            P("gx", "gy", None),
            P("gx", "gy", None),
            P("gx", "gy", None),
            P("gx", "gy", None),
        ),
        out_specs=(P("grp", "gx", "gy", None), P(("grp", "gx", "gy"))),
        check_vma=False,
    )
```

```python
import jax
import jax.numpy as jnp
from jax import lax
from jax.experimental import pallas as pl
from jax.experimental.pallas import tpu as pltpu
from jax.sharding import PartitionSpec as P

MESH = pl.DeviceIdType.MESH
F32 = jnp.float32
YN, ZLN, ZHN, XN = 4, 4, 2, 4
NGX, NGY = YN * ZLN, ZHN * XN
ZN, CN = ZLN * ZHN, YN * XN
CX, CY, CZ = 8, 32, 512
KT = CZ // 128
Y0 = 8
YP = 48
PAD = (CX, KT, YP, 128)
FLAT = (CX, KT, CY, 128)
ND_DEV = 64
OUTSIDE = -0.25
ROWS = pl.ds(Y0, CY)
VIEWS = True

Z_STEPS = sorted(range(1, ZN), key=lambda d: -min(d, ZN - d))
PLANE_STEPS = sorted(
    ((dy, dx) for dy in range(YN) for dx in range(XN) if dy or dx),
    key=lambda o: -min(o[0], YN - o[0]) - min(o[1], XN - o[1]),
)

A_V0, A_Q, A_L2, A_V1, A_L1 = range(5)
R_BULK, R_O1, R_O2, R_D1, R_D2, R_QX, R_QY = range(20, 27)
N_RECV = 27
N_SEND = 48


def kernel(
    fields, stored, por, lab, heat, own,
    out, sens,
    V0, V1, KA, KB, KR, Q, L2, L1, RES, W0, WP, WM,
    S0, LB, PR, HT,
    HX, HY, FY, UX, UY,
    OB, ocol, otab, drow, dmix, dcol, dtab, acc, sel, rsel,
    ssem, rsem, dsem, lsem, ready,
):
    grp = lax.axis_index("grp")
    gx = lax.axis_index("gx")
    gy = lax.axis_index("gy")
    fwd = grp == 0
    adj = grp == 1
    yy, zl = lax.div(gx, ZLN), lax.rem(gx, ZLN)
    zh, xx = lax.div(gy, XN), lax.rem(gy, XN)
    zz = zh * ZLN + zl
    cc = yy * XN + xx
    has = (gx > 0, gx < NGX - 1, gy > 0, gy < NGY - 1)
    sends_to = (has[1], has[0], has[3], has[2])

    def device(g, step):
        dx, dy = ((1, 0), (-1, 0), (0, 1), (0, -1))[step]
        return {"grp": g, "gx": lax.rem(gx + dx + NGX, NGX), "gy": lax.rem(gy + dy + NGY, NGY)}

    def column(g, y, x, z):
        return {"grp": g, "gx": y * ZLN + lax.rem(z, ZLN), "gy": lax.div(z, ZLN) * XN + x}

    def z_peer(d):
        return column(grp, yy, xx, lax.rem(zz + d, ZN))

    def plane_peer(g, o):
        return {"grp": g, "gx": lax.rem(yy + o[0], YN) * ZLN + zl, "gy": zh * XN + lax.rem(xx + o[1], XN)}

    partner = {"grp": 1 - grp, "gx": gx, "gy": gy}
    y_up, y_down = lax.rem(yy + 1, YN), lax.rem(yy + YN - 1, YN)
    x_up, x_down = lax.rem(xx + 1, XN), lax.rem(xx + XN - 1, XN)

    bar = pltpu.get_barrier_semaphore()

    def tell(dev):
        pl.semaphore_signal(bar, inc=1, device_id=dev, device_id_type=MESH)

    for s in (2, 3, 0, 1):

        @pl.when(sends_to[s])
        def _():
            tell(device(grp, s))

        @pl.when(jnp.logical_and(adj, sends_to[s]))
        def _():
            tell(device(0, s))

    tell(partner)

    def load(src, dst, slot):
        copies = [
            pltpu.make_async_copy(src.at[:, :, pl.ds(128 * k, 128)], dst(k), lsem.at[slot, k])
            for k in range(KT)
        ]
        for c in copies:
            c.start()
        return copies

    ld_stored = load(stored.at[0], lambda k: S0.at[:, k], 0)
    ld_lab = load(lab, lambda k: LB.at[:, k], 1)
    ld_por = load(por, lambda k: PR.at[:, k], 2)

    def fields_copies(dst):
        return [
            pltpu.make_async_copy(
                fields.at[0, :, :, pl.ds(128 * k, 128)], dst.at[:, k, ROWS, :], lsem.at[3, k]
            )
            for k in range(KT)
        ]

    @pl.when(fwd)
    def _():
        for c in fields_copies(V0):
            c.start()

    @pl.when(adj)
    def _():
        for c in fields_copies(L2):
            c.start()

    ld_heat = load(heat, lambda k: HT.at[:, k], 4)
    ld_own = pltpu.make_async_copy(own.at[0, pl.ds(0, 8), :], OB, lsem.at[5, 0])
    ld_own.start()

    for d in Z_STEPS:
        tell(z_peer(d))
    for o in PLANE_STEPS:
        tell(plane_peer(grp, o))

    @pl.when(fwd)
    def _():
        for o in PLANE_STEPS:
            tell(plane_peer(1, o))

    near = sum(h.astype(jnp.int32) for h in has)
    bottom, top = zl == 0, zl == ZLN - 1
    told = ZN - 1 + CN - 1 + 1
    expected = jnp.where(fwd, 2 * near + told, near + told + CN - 1)

    sub = lax.broadcasted_iota(jnp.int32, (KT, 8, 128), 1)
    lane4 = lax.broadcasted_iota(jnp.int32, (KT, 8, 128), 2)

    def z_next(x):
        r = pltpu.roll(x, 127, 2)
        after = jnp.concatenate([r[1:], jnp.zeros_like(r[:1])], axis=0)
        return jnp.where(lane4 == 127, after, r)

    def z_back(x, edge):
        r = pltpu.roll(x, 1, 2)
        before = jnp.concatenate([edge[None], r[:-1]], axis=0)
        return jnp.where(lane4 == 0, before, r)

    def at(ref, i, y):
        return ref[i, :, pl.ds(y, 8), :]

    def flat_at(ref, i, g):
        return ref[i, :, pl.ds(8 * g, 8), :]

    def around(ref, i, g, here):
        y = Y0 + 8 * g
        above, below = at(ref, i, y + 1), at(ref, i, y - 1)
        if g == CY // 8 - 1:
            above = jnp.where(sub == 7, here, above)
        if g == 0:
            below = jnp.where(sub == 0, here, below)
        return at(ref, jnp.minimum(i + 1, CX - 1), y), at(ref, jnp.maximum(i - 1, 0), y), above, below

    def sweep(body, init=0):
        return lax.fori_loop(0, CX, body, init)

    LAYER = (CX - 1, 0)
    ROW = (CY - 1, 0)
    SIDE_LAYER = (0, CX - 1)
    SIDE_ROW = (0, CY - 1)

    def get_lines(ref, row, pitch=YP, first=Y0):
        if not VIEWS:
            return jnp.stack([ref[:, k, first + row, :] for k in range(KT)], axis=0)
        flat = ref.reshape(CX * KT * pitch, 128)
        return jnp.stack(
            [flat[pl.ds(k * pitch + first + row, CX, stride=KT * pitch), :] for k in range(KT)], axis=0
        )

    def put_lines(ref, row, x, pitch=YP, first=Y0):
        for k in range(KT):
            if VIEWS:
                flat = ref.reshape(CX * KT * pitch, 128)
                flat[pl.ds(k * pitch + first + row, CX, stride=KT * pitch), :] = x[k]
            else:
                ref[:, k, first + row, :] = x[k]

    def layer(ref, i):
        return ref[i, :, ROWS, :]

    def conduct(q, v):
        return 0.2 + q * (0.8 + 0.1 * v)

    def conductivity(V, K):
        def body(i, _):
            K[i, :, ROWS, :] = conduct(Q[i, :, ROWS, :], V[i, :, ROWS, :])
            return 0

        sweep(body)

    for s in range(4):

        @pl.when(jnp.logical_not(has[s]))
        def _():
            for a in (A_V0, A_L2, A_V1, A_L1):
                if s < 2:
                    HX[a, s] = jnp.zeros((KT, CY, 128), F32)
                else:
                    HY[a, s - 2] = jnp.zeros((KT, CX, 128), F32)

        @pl.when(jnp.logical_and(adj, jnp.logical_not(has[s])))
        def _():
            if s < 2:
                HX[A_Q, s] = jnp.full((KT, CY, 128), OUTSIDE, F32)
            else:
                HY[A_Q, s - 2] = jnp.full((KT, CX, 128), OUTSIDE, F32)

    for c in ld_lab + ld_por:
        c.wait()

    def solid_share(i, _):
        label = LB[i]
        Q[i, :, ROWS, :] = jnp.where(label == 0, 1.0, jnp.where(label == 1, 0.0, PR[i]))
        return 0

    sweep(solid_share)
    for c in ld_stored:
        c.wait()
    for s in range(2):
        FY[A_Q, s] = get_lines(Q, ROW[s])

    @pl.when(fwd)
    def _():
        for s in range(2):
            FY[A_L2, s] = get_lines(S0, ROW[s], CY, 0)
        for c in fields_copies(V0):
            c.wait()
        for s in range(2):
            FY[A_V0, s] = get_lines(V0, ROW[s])

    @pl.when(adj)
    def _():
        for c in fields_copies(L2):
            c.wait()
        for s in range(2):
            FY[A_L2, s] = get_lines(L2, ROW[s])

    ld_own.wait()
    lane = lax.broadcasted_iota(jnp.int32, (1, 128), 1)
    quarter = lax.rem(lane, KT)
    ids = jnp.zeros((1, 128), jnp.int32)
    for k in range(KT):
        ids = jnp.where(quarter == k, OB[0:1, 128 * k : 128 * k + 128], ids)
    if ZN < 8:
        dcol[...] = jnp.zeros((8, 128), F32)
    ocol[pl.ds(zz, 1), :] = ids

    sent = []

    def remote(cond, src, dst, dev, recv):
        slot = len(sent)

        def make():
            return pltpu.make_async_remote_copy(
                src_ref=src, dst_ref=dst, send_sem=ssem.at[slot], recv_sem=rsem.at[recv],
                device_id=dev, device_id_type=MESH,
            )

        @pl.when(cond)
        def _():
            make().start()

        sent.append((cond, make))

    def arrive(cond, dst, recv):
        @pl.when(cond)
        def _():
            pltpu.make_async_copy(dst, dst, rsem.at[recv]).wait()

    def rim(a, s):
        return HX.at[a, s] if s < 2 else HY.at[a, s - 2]

    def send_faces(cond, g, a, layers, edge):
        for s in (2, 3, 0, 1):
            src = layers(LAYER[s]) if s < 2 else FY.at[edge, s - 2]
            remote(jnp.logical_and(cond, sends_to[s]), src, rim(a, s), device(g, s), 4 * a + s)

    def faces_arrive(cond, a):
        for s in range(4):
            arrive(jnp.logical_and(cond, has[s]), rim(a, s), 4 * a + s)

    def both(ref):
        return lambda i: ref.at[i, :, ROWS, :]

    pl.semaphore_wait(bar, expected)
    send_faces(fwd, 1, A_V0, lambda i: S0.at[i], A_L2)
    remote(fwd, S0, V0.at[:, :, ROWS, :], partner, R_BULK)
    send_faces(adj, 1, A_Q, both(Q), A_Q)

    def spread(src, dst, sem, rsm, peers):
        for dev in peers:
            pltpu.make_async_remote_copy(
                src_ref=src, dst_ref=dst, send_sem=sem, recv_sem=rsm,
                device_id=dev, device_id_type=MESH,
            ).start()

    @pl.when(adj)
    def _():
        for o in ((0, 1), (0, XN - 1), (1, 0), (YN - 1, 0)):
            pl.semaphore_signal(ready, inc=1, device_id=plane_peer(1, o), device_id_type=MESH)

    here = ocol.at[pl.ds(zz, 1), :]
    spread(here, here, dsem.at[0], rsem.at[R_O1], [z_peer(d) for d in Z_STEPS])

    for c in ld_heat:
        c.wait()

    def advance(V, K, out_ref):
        def body(i, _):
            for g in range(CY // 8):
                y = Y0 + 8 * g
                v, k = at(V, i, y), at(K, i, y)
                flux = jnp.zeros_like(v)
                for vn, kn in zip(around(V, i, g, v), around(K, i, g, k)):
                    flux += (k + kn) * (vn - v)
                up = (k + z_next(k)) * (z_next(v) - v)
                flux += up - z_back(up, k[0] * v[0])
                q = at(Q, i, y)
                out_ref[i, :, pl.ds(y, 8), :] = v + 0.04 * (flux - v + q * v) + 0.08 * flat_at(HT, i, g)
            return 0

        sweep(body)

    def advance_rims(V, K, a, out_ref):
        for s in range(2):
            i = SIDE_LAYER[s]
            vn, qn = HX[a, s], HX[A_Q, s]
            flux = (layer(K, i) + conduct(qn, vn)) * (vn - layer(V, i))
            out_ref[i, :, ROWS, :] = layer(out_ref, i) + 0.04 * flux
        for s in range(2):
            j = SIDE_ROW[s]
            vn, qn, v = HY[a, s], HY[A_Q, s], get_lines(V, j)
            flux = (conduct(get_lines(Q, j), v) + conduct(qn, vn)) * (vn - v)
            put_lines(out_ref, j, get_lines(out_ref, j) + 0.04 * flux)

    def porous_at(i, g):
        return jnp.where(flat_at(LB, i, g) == 2, 0.04, 0.0)

    arrive(adj, V0.at[:, :, ROWS, :], R_BULK)
    conductivity(V0, KA)
    advance(V0, KA, V1)
    send_faces(adj, 1, A_L2, both(L2), A_L2)
    send_faces(fwd, 0, A_V0, both(V0), A_V0)

    @pl.when(adj)
    def _():
        def rates(i, _):
            KR[i, :, ROWS, :] = jnp.where(LB[i] == 2, 0.04, 0.0) * (0.8 + 0.1 * V0[i, :, ROWS, :])
            return 0

        sweep(rates)

        def weights(i, _):
            for g in range(CY // 8):
                y = Y0 + 8 * g
                v, r = at(V0, i, y), at(KR, i, y)
                w = porous_at(i, g) * v
                for vn, rn in zip(around(V0, i, g, v), around(KR, i, g, r)):
                    w += (r + rn) * (vn - v)
                dz = z_next(v) - v
                W0[i, :, pl.ds(8 * g, 8), :] = w + r * (dz - z_back(dz, v[0]))
                WP[i, :, pl.ds(8 * g, 8), :] = -z_back(r * dz, jnp.zeros((8, 128), F32))
                WM[i, :, pl.ds(8 * g, 8), :] = z_next(r) * dz
            return 0

        sweep(weights)

    def rows_of(n, sem):
        return pltpu.make_async_copy(dmix.at[pl.ds(0, n)], dmix.at[pl.ds(0, n)], sem)

    rows_of(ZN - 1, rsem.at[R_O1]).wait()
    otab[cc] = ocol[...]
    spread(ocol, otab.at[cc], dsem.at[1], rsem.at[R_O2], [plane_peer(grp, o) for o in PLANE_STEPS])

    faces_arrive(adj, A_Q)
    remote(adj, HX.at[A_Q], HX.at[A_Q], partner, R_QX)
    remote(adj, HY.at[A_Q], HY.at[A_Q], partner, R_QY)
    arrive(fwd, HX.at[A_Q], R_QX)
    arrive(fwd, HY.at[A_Q], R_QY)
    faces_arrive(grp >= 0, A_V0)
    advance_rims(V0, KA, A_V0, V1)

    for s in range(2):
        FY[A_V1, s] = get_lines(V1, ROW[s])
    send_faces(grp >= 0, grp, A_V1, both(V1), A_V1)

    conductivity(V1, KB)

    @pl.when(fwd)
    def _():
        advance(V1, KB, RES)

    def retreat(V, K, L, out_ref, sums):
        def body(i, total):
            for g in range(CY // 8):
                y = Y0 + 8 * g
                v, k, l = at(V, i, y), at(K, i, y), at(L, i, y)
                ss = jnp.zeros_like(v)
                tt = jnp.zeros_like(v)
                for vn, kn, ln in zip(around(V, i, g, v), around(K, i, g, k), around(L, i, g, l)):
                    jump = l - ln
                    ss += (vn - v) * jump
                    tt += (k + kn) * jump
                jump = l - z_next(l)
                s = (z_next(v) - v) * jump
                t = (k + z_next(k)) * jump
                ss += s + z_back(s, -v[0] * l[0])
                tt += t - z_back(t, -k[0] * l[0])
                q = at(Q, i, y)
                out_ref[i, :, pl.ds(y, 8), :] = (
                    l + 0.04 * (0.1 * q * ss - tt - l + q * l) + (v - flat_at(S0, i, g))
                )
                if sums:
                    total = total + porous_at(i, g) * ((0.8 + 0.1 * v) * ss + v * l)
            return total

        return sweep(body, jnp.zeros((KT, 8, 128), F32))

    def retreat_rims(V, K, av, L, al, out_ref, sums):
        for s in range(2):
            i = SIDE_LAYER[s]
            v, l, vn = layer(V, i), layer(L, i), HX[av, s]
            jump = l - HX[al, s]
            ss = (vn - v) * jump
            tt = (layer(K, i) + conduct(HX[A_Q, s], vn)) * jump
            out_ref[i, :, ROWS, :] = layer(out_ref, i) + 0.04 * (0.1 * layer(Q, i) * ss - tt)
            if sums:
                x = jnp.where(LB[i] == 2, 0.04, 0.0) * (0.8 + 0.1 * v) * ss
                acc[0] += sum(x[:, 8 * g : 8 * g + 8] for g in range(CY // 8))
        for s in range(2):
            j = SIDE_ROW[s]
            v, l, q, vn = get_lines(V, j), get_lines(L, j), get_lines(Q, j), HY[av, s]
            jump = l - HY[al, s]
            ss = (vn - v) * jump
            tt = (conduct(q, v) + conduct(HY[A_Q, s], vn)) * jump
            put_lines(out_ref, j, get_lines(out_ref, j) + 0.04 * (0.1 * q * ss - tt))
            if sums:
                acc[0] += jnp.where(get_lines(LB, j, CY, 0) == 2, 0.04, 0.0) * (0.8 + 0.1 * v) * ss

    @pl.when(adj)
    def _():
        acc[0] = retreat(V1, KB, L2, L1, True)
        for s in range(2):
            i = SIDE_LAYER[s]
            v, vn, qn = layer(V0, i), HX[A_V0, s], HX[A_Q, s]
            W0[i] = W0[i] + layer(KR, i) * (vn - v)
            inside = jnp.logical_and(qn > 0.0, qn < 1.0)
            UX[s] = jnp.where(inside, 0.04, 0.0) * (0.8 + 0.1 * vn) * (vn - v)
        for s in range(2):
            j = SIDE_ROW[s]
            v, vn, qn = get_lines(V0, j), HY[A_V0, s], HY[A_Q, s]
            put_lines(W0, j, get_lines(W0, j, CY, 0) + get_lines(KR, j) * (vn - v), CY, 0)
            inside = jnp.logical_and(qn > 0.0, qn < 1.0)
            UY[s] = jnp.where(inside, 0.04, 0.0) * (0.8 + 0.1 * vn) * (vn - v)

    faces_arrive(grp >= 0, A_V1)

    @pl.when(fwd)
    def _():
        advance_rims(V1, KB, A_V1, RES)

    faces_arrive(adj, A_L2)

    @pl.when(adj)
    def _():
        retreat_rims(V1, KB, A_V1, L2, A_L2, L1, True)
        for s in range(2):
            FY[A_L1, s] = get_lines(L1, ROW[s])

        def weigh(i, totals):
            r0, rp, rm = totals
            for g in range(CY // 8):
                l = at(L1, i, Y0 + 8 * g)
                r0 = r0 + flat_at(W0, i, g) * l
                rp = rp + flat_at(WP, i, g) * l
                rm = rm + flat_at(WM, i, g) * l
            return r0, rp, rm

        zero = jnp.zeros((KT, 8, 128), F32)
        r0, rp, rm = sweep(weigh, (acc[0], zero, zero))
        own_sum = r0 + z_next(rp) + z_back(rm, jnp.zeros((8, 128), F32))
        parts = [own_sum]
        for s in (1, 0):
            x = UX[s] * layer(L1, SIDE_LAYER[s])
            parts.append(sum(x[:, 8 * g : 8 * g + 8] for g in range(CY // 8)))
        for s in (1, 0):
            parts.append(UY[s] * get_lines(L1, SIDE_ROW[s]))
        mixed = jnp.zeros((KT, 8, 128), F32)
        for n, x in enumerate(parts):
            mixed = jnp.where(sub == n, jnp.sum(x, axis=1, keepdims=True), mixed)
        lanes8 = lax.rem(lax.broadcasted_iota(jnp.int32, (8, 128), 1), KT)
        sums = jnp.zeros((8, 128), F32)
        for k in range(KT):
            x = mixed[k]
            total = x
            for i in range(KT):
                if i != k:
                    total = total + pltpu.roll(x, (k - i) % 128, 1)
            sums = jnp.where(lanes8 == k, total, sums)
        drow[...] = sums
        dmix[pl.ds(zz, 1), :] = drow[0:1]

        def scatter(kind, y, x, target, first):
            src, dst = drow.at[pl.ds(kind, 1), :], dmix.at[pl.ds(kind * ZN + target, 1), :]
            spread(
                src, dst, dsem.at[2], rsem.at[R_D1],
                [column(1, y, x, lax.rem(zz + d, ZN)) for d in Z_STEPS + [0] * (1 - first)],
            )

        pl.semaphore_wait(ready, 4)
        z_up, z_down = lax.rem(zz + 1, ZN), lax.rem(zz + ZN - 1, ZN)
        flip = lax.rem(zz + ZLN * (ZHN - 1), ZN)
        lo_z, hi_z = zh * ZLN, zh * ZLN + ZLN - 1
        scatter(3, yy, x_up, jnp.where(xx == XN - 1, flip, zz), 0)
        scatter(4, yy, x_down, jnp.where(xx == 0, flip, zz), 0)
        scatter(0, yy, xx, zz, 1)
        y_to, z_to = jnp.where(top, y_up, yy), jnp.where(top, lo_z, z_up)
        scatter(1, y_to, xx, z_to, 1)
        y_from, z_from = jnp.where(bottom, y_down, yy), jnp.where(bottom, hi_z, z_down)
        scatter(2, y_from, xx, z_from, 1)

        def one(kind, y, target):
            pltpu.make_async_remote_copy(
                src_ref=drow.at[pl.ds(kind, 1), :], dst_ref=dmix.at[pl.ds(kind * ZN + target, 1), :],
                send_sem=dsem.at[2], recv_sem=rsem.at[R_D1],
                device_id=column(1, y, xx, zz), device_id_type=MESH,
            ).start()

        @pl.when(top)
        def _():
            one(1, y_up, lo_z)

        @pl.when(jnp.logical_not(top))
        def _():
            dmix[pl.ds(ZN + z_up, 1), :] = drow[1:2]

        @pl.when(bottom)
        def _():
            one(2, y_down, hi_z)

        @pl.when(jnp.logical_not(bottom))
        def _():
            dmix[pl.ds(2 * ZN + z_down, 1), :] = drow[2:3]

    send_faces(adj, 1, A_L1, both(L1), A_L1)

    def mixed_wait(sem):
        middle = jnp.logical_not(jnp.logical_or(bottom, top))

        @pl.when(middle)
        def _():
            rows_of(5 * ZN - 3, sem).wait()

        @pl.when(jnp.logical_not(middle))
        def _():
            rows_of(5 * ZN - 2, sem).wait()

    @pl.when(adj)
    def _():
        retreat(V0, KA, L1, RES, False)

    def tables(ref, n, sem):
        return pltpu.make_async_copy(ref.at[pl.ds(0, n)], ref.at[pl.ds(0, n)], sem)

    tables(otab, CN - 1, rsem.at[R_O2]).wait()
    base = (grp * NGX * NGY + gx * NGY + gy) * ND_DEV
    place = (
        lax.broadcasted_iota(jnp.int32, (CN, 8, 128), 0) * 8
        + lax.broadcasted_iota(jnp.int32, (CN, 8, 128), 1)
        + 1
    ).astype(F32)

    def find(j, _):
        hit = otab[...] == base + j
        rsel[pl.ds(j, 1), :] = jnp.sum(jnp.sum(jnp.where(hit, place, 0.0), axis=0), axis=0, keepdims=True)
        return 0

    lax.fori_loop(0, ND_DEV, find, 0)
    row_at = jnp.sum(rsel[...], axis=1, keepdims=True)
    spot = lax.broadcasted_iota(jnp.int32, (ND_DEV, CN * 8), 1).astype(F32)
    sel[...] = jnp.where(row_at == spot + 1.0, 1.0, 0.0).astype(jnp.bfloat16)

    @pl.when(adj)
    def _():
        mixed_wait(rsem.at[R_D1])
        total = dmix[pl.ds(0, ZN), :]
        for n in range(1, 5):
            total = total + dmix[pl.ds(n * ZN, ZN), :]
        dcol[pl.ds(0, ZN), :] = total
        dtab[cc] = dcol[...]
        spread(
            dcol, dtab.at[cc], dsem.at[3], rsem.at[R_D2],
            [plane_peer(g, o) for o in PLANE_STEPS for g in (1, 0)] + [partner],
        )

    faces_arrive(adj, A_L1)

    @pl.when(adj)
    def _():
        retreat_rims(V0, KA, A_V0, L1, A_L1, RES, False)

    def result(i, _):
        for k in range(KT):
            out[0, i, :, 128 * k : 128 * k + 128] = RES[i, k, ROWS, :]
        return 0

    sweep(result)

    @pl.when(fwd)
    def _():
        tables(dtab, CN, rsem.at[R_D2]).wait()

    @pl.when(adj)
    def _():
        tables(dtab, CN - 1, rsem.at[R_D2]).wait()

    table = dtab[...].reshape(CN * 8, 128)
    high = table.astype(jnp.bfloat16)
    rest = table - high.astype(F32)
    middle = rest.astype(jnp.bfloat16)
    low = (rest - middle.astype(F32)).astype(jnp.bfloat16)
    thirds = jnp.dot(sel[...], jnp.concatenate([high, middle, low], axis=1), preferred_element_type=F32)
    picked = (thirds[:, :128] + thirds[:, 128:256]) + thirds[:, 256:]
    each = jnp.sum(jnp.where(rsel[...] > 0.0, picked, 0.0), axis=1, keepdims=True)
    row = lax.broadcasted_iota(jnp.int32, (ND_DEV, 128), 0)
    col = lax.broadcasted_iota(jnp.int32, (ND_DEV, 128), 1)
    sens[...] = jnp.sum(jnp.where(row == col, each, 0.0), axis=0)[:ND_DEV]

    for cond, make in sent:

        @pl.when(cond)
        def _():
            make().wait_send()

    rows_of(ZN - 1, dsem.at[0]).wait()
    tables(otab, CN - 1, dsem.at[1]).wait()

    @pl.when(adj)
    def _():
        mixed_wait(dsem.at[2])
        tables(dtab, CN - 1, dsem.at[3]).wait()
        tables(dtab, CN, dsem.at[3]).wait()


def hand_over(field, sums, field_out, sums_out, sem):
    a = pltpu.make_async_copy(field, field_out, sem.at[0])
    b = pltpu.make_async_copy(sums, sums_out, sem.at[1])
    a.start()
    b.start()
    a.wait()
    b.wait()


def shards(fields, stored, porosity, labels, heat_source, design_owner):
    anywhere = pl.BlockSpec(memory_space=pl.ANY)
    here = pl.BlockSpec(memory_space=pltpu.VMEM)
    pad = pltpu.VMEM(PAD, F32)
    flat = pltpu.VMEM(FLAT, F32)
    out, sens = pl.pallas_call(
        kernel,
        out_shape=(pltpu.VMEM((1, CX, CY, CZ), F32), pltpu.VMEM((ND_DEV,), F32)),
        in_specs=[anywhere] * 6,
        out_specs=(here, here),
        scratch_shapes=[pad] * 9 + [flat] * 3 + [
            flat, pltpu.VMEM(FLAT, jnp.int32), flat, flat,
            pltpu.VMEM((5, 2, KT, CY, 128), F32), pltpu.VMEM((5, 2, KT, CX, 128), F32),
            pltpu.VMEM((5, 2, KT, CX, 128), F32),
            pltpu.VMEM((2, KT, CY, 128), F32), pltpu.VMEM((2, KT, CX, 128), F32),
            pltpu.VMEM((8, CZ), jnp.int32),
            pltpu.VMEM((8, 128), jnp.int32), pltpu.VMEM((CN, 8, 128), jnp.int32),
            pltpu.VMEM((8, 128), F32), pltpu.VMEM((5 * 8, 128), F32),
            pltpu.VMEM((8, 128), F32), pltpu.VMEM((CN, 8, 128), F32),
            pltpu.VMEM((1, KT, 8, 128), F32),
            pltpu.VMEM((ND_DEV, CN * 8), jnp.bfloat16), pltpu.VMEM((ND_DEV, 128), F32),
            pltpu.SemaphoreType.DMA((N_SEND,)),
            pltpu.SemaphoreType.DMA((N_RECV,)),
            pltpu.SemaphoreType.DMA((4,)),
            pltpu.SemaphoreType.DMA((7, KT)),
            pltpu.SemaphoreType.REGULAR,
        ],
        compiler_params=pltpu.CompilerParams(collective_id=0, has_side_effects=True),
    )(fields, stored, porosity, labels, heat_source, design_owner)
    return pl.pallas_call(
        hand_over,
        out_shape=(jax.ShapeDtypeStruct((1, CX, CY, CZ), F32), jax.ShapeDtypeStruct((ND_DEV,), F32)),
        in_specs=[here, here],
        out_specs=(anywhere, anywhere),
        scratch_shapes=[pltpu.SemaphoreType.DMA((2,))],
    )(pltpu.with_memory_space_constraint(out, pltpu.VMEM), pltpu.with_memory_space_constraint(sens, pltpu.VMEM))


def solution(mesh):
    return jax.shard_map(
        shards,
        mesh=mesh,
        in_specs=(
            P("grp", "gx", "gy", None),
            P("grp", "gx", "gy", None),
            P("gx", "gy", None),
            P("gx", "gy", None),
            P("gx", "gy", None),
            P("gx", "gy", None),
        ),
        out_specs=(P("grp", "gx", "gy", None), P(("grp", "gx", "gy"))),
        check_vma=False,
    )
```
